512 devices in a mesh: lon: 16 (over y, x_lo, core), lat: 32 (over x_hi, z).
Axes of the slice: x: 4 (x_hi: 2, x_lo: 2; x = x_hi * 2 + x_lo), y: 4, z: 16, core: 2. Of those that a mesh axis runs over, the one named last changes fastest.
Arguments:
- tokens: bfloat16 [256, 256, 768], P('lat', 'lon'), may hold values from -6 to 6
- patch_valid: int32 [256, 256], P('lat', 'lon'), may hold values 0 or 1
- block_mask: int32 [32, 16, 16], P('lat', 'lon'), may hold values from 0 to 1, as said below
- gain_attn: float32 [768], replicated, may hold values from 0.1 to 1.9
- gain_mlp: float32 [768], replicated, may hold values from 0.1 to 1.9
- w_qkv: bfloat16 [768, 2304], P('lat'), may hold values from -1.5 to 1.5
- w_out: bfloat16 [768, 768], P('lat'), may hold values from -0.21875 to 0.21875
- w_up: bfloat16 [768, 1536], P('lat'), may hold values from -0.21875 to 0.21875
- w_down: bfloat16 [1536, 768], P('lat'), may hold values from -0.15625 to 0.15625
Outputs:
- mixed: bfloat16 [256, 256, 768], P('lat', 'lon')
The draws below stay inside these ranges and needn't reach their ends.
Inputs may be any that keep to these rules, and one draw needn't show every extreme that they name: block_mask[s, b, b] is 1 for every strip s and band b.
All inputs are finite; a program needn't handle non-finite values. No bound on the sum of `patch_valid` on one device may be relied on, other than what follows from the above.
Results may differ from the reference program's by a relative error of at most 0.013.
Values may be sent and summed in bfloat16 or wider, within the bound.
No kernel may reach another device: no remote copies, remote signals or barrier semaphores. Data moves between devices by JAX's collectives and lax.ppermute only.
A program may use at most 64 MiB of HBM per device.

```python
import jax
import jax.numpy as jnp
from jax import lax

D = 768
HEADS = 12
HEAD = 64
FFW = 1536
HALO = 2
TLAT = 8
TLON = 16
TOKD = 128
NLAT = 256
NLON = 256
N_LON = 16
N_LAT = 32


def draw_tokens(key, part):
    first = jax.random.fold_in(key, 0)
    result = jax.random.normal(first, (NLAT, NLON, D), jnp.float32)
    return jnp.clip(result, -6.0, 6.0).astype(jnp.bfloat16)


def draw_block_mask(key, part):
    first, second = jax.random.split(jax.random.fold_in(key, 11))
    levels = jax.random.randint(first, (N_LAT, 1, 1), 1, 9)
    rolls = jax.random.randint(second, (N_LAT, N_LON, N_LON), 0, 8)
    ocean = (rolls < levels).astype(jnp.int32)
    diagonal = (lax.broadcasted_iota(jnp.int32, (N_LAT, N_LON, N_LON), 1) == lax.broadcasted_iota(jnp.int32, (N_LAT, N_LON, N_LON), 2)).astype(jnp.int32)
    return jnp.maximum(ocean, diagonal)


def draw_w_qkv(key, part):
    first, second, third = jax.random.split(jax.random.fold_in(key, 23), 3)
    scale = D ** (-0.5)
    values = jax.random.normal(third, (D, D), jnp.float32) * scale
    query_part = jax.random.normal(first, (D, D), jnp.float32) * (2.0 * scale)
    key_part = jax.random.normal(second, (D, D), jnp.float32) * (2.0 * scale)
    result = jnp.concatenate([query_part, key_part, values], axis=1)
    return jnp.clip(result, -1.5, 1.5).astype(jnp.bfloat16)


def with_ends(values, key, low, largest):
    index_at = [jax.random.randint(jax.random.fold_in(key, axis), (), 0, length) for axis, length in enumerate(values.shape)]
    widest = values.shape.index(max(values.shape))
    beside = index_at[:widest] + [(index_at[widest] + 1) % values.shape[widest]] + index_at[widest + 1:]
    return values.at[tuple(index_at)].set(low).at[tuple(beside)].set(largest)


def block_levels(rng, dims, cuts, least, high):
    gain, own = 1.0, jax.random.fold_in(rng, 6)
    for axis_at, blocks in cuts:
        draws = jnp.exp(jax.random.uniform(jax.random.fold_in(own, axis_at), (blocks,), jnp.float32, least / len(cuts), high / len(cuts)))
        gain = gain * jnp.repeat(draws, dims[axis_at] // blocks).reshape([-1 if axis == axis_at else 1 for axis in range(len(dims))])
    return gain


def bell_draw(rng, extent, scale, limit, shards=(), kind=jnp.bfloat16):
    values = scale * jax.random.normal(rng, extent, jnp.float32)
    if shards:
        values = values * block_levels(rng, extent, shards, -0.22, 0.18)
    return jnp.clip(values, -limit, limit).astype(kind)


def setup_inputs(seed: int = 0) -> dict:
    keys = jax.random.split(jax.random.key(seed), 10)
    return {
        "tokens": draw_tokens(jax.random.fold_in(keys[9], 71), 0),
        "patch_valid": with_ends((jax.random.randint(keys[1], (NLAT, NLON), 0, 4) < 3).astype(jnp.int32), jax.random.fold_in(keys[1], 1), 0, 1),
        "block_mask": draw_block_mask(jax.random.fold_in(keys[9], 71), 0),
        "gain_attn": jnp.clip(1.0 + 0.18 * jax.random.normal(keys[3], (D,), jnp.float32), 0.1, 1.9),
        "gain_mlp": jnp.clip(1.0 + 0.18 * jax.random.normal(keys[4], (D,), jnp.float32), 0.1, 1.9),
        "w_qkv": draw_w_qkv(jax.random.fold_in(keys[9], 71), 0),
        "w_out": bell_draw(keys[6], (D, D), D ** -0.5, 0.21875, ((0, 32),)),
        "w_up": bell_draw(keys[7], (D, FFW), D ** -0.5, 0.21875, ((0, 32),)),
        "w_down": bell_draw(keys[8], (FFW, D), FFW ** -0.5, 0.15625, ((0, 32),)),
    }


MASKED = -1e+30

def layer_norm(inputs, gain_vec):
    centre = lax.optimization_barrier(jnp.mean(inputs, axis=-1, keepdims=True))
    spread = lax.optimization_barrier(jnp.mean((inputs - centre) ** 2, axis=-1, keepdims=True))
    return (inputs - centre) * lax.rsqrt(spread + 1e-05) * gain_vec

def reference(tokens, patch_valid, block_mask, gain_attn, gain_mlp, w_qkv, w_out, w_up, w_down):
    count_all = NLAT * NLON
    flattened = tokens.reshape(count_all, D).astype(jnp.float32)
    normed = layer_norm(flattened, gain_attn).astype(jnp.bfloat16)
    projected = jnp.dot(normed, w_qkv, preferred_element_type=jnp.float32)
    queries = (projected[:, :D] * HEAD ** (-0.5)).astype(jnp.bfloat16).reshape(NLAT, NLON, HEADS, HEAD)
    key_grid = projected[:, D:2 * D].astype(jnp.bfloat16).reshape(NLAT, NLON, HEADS, HEAD)
    value_grid = projected[:, 2 * D:].astype(jnp.bfloat16).reshape(NLAT, NLON, HEADS, HEAD)
    padding = ((HALO, HALO), (0, 0), (0, 0), (0, 0))
    key_padded = jnp.pad(key_grid, padding)
    value_padded = jnp.pad(value_grid, padding)
    mask_rows = block_mask.reshape(N_LAT * N_LON, N_LON)
    column_band = (jnp.arange(NLON, dtype=jnp.int32) // TLON).astype(jnp.int32)
    zero_index = jnp.zeros((), jnp.int32)

    def tile(tile_index):
        strip_index = (tile_index // N_LON).astype(jnp.int32)
        band_index = (tile_index % N_LON).astype(jnp.int32)
        row_first = (strip_index * TLAT).astype(jnp.int32)
        col_first = (band_index * TLON).astype(jnp.int32)
        query_tile = lax.dynamic_slice(queries, (row_first, col_first, zero_index, zero_index), (TLAT, TLON, HEADS, HEAD)).reshape(TOKD, HEADS, HEAD)
        strip_keys = lax.dynamic_slice(key_grid, (row_first, zero_index, zero_index, zero_index), (TLAT, NLON, HEADS, HEAD)).reshape(TLAT * NLON, HEADS, HEAD)
        strip_values = lax.dynamic_slice(value_grid, (row_first, zero_index, zero_index, zero_index), (TLAT, NLON, HEADS, HEAD)).reshape(TLAT * NLON, HEADS, HEAD)
        below_first = (row_first + TLAT + HALO).astype(jnp.int32)
        above_keys = lax.dynamic_slice(key_padded, (row_first, col_first, zero_index, zero_index), (HALO, TLON, HEADS, HEAD)).reshape(HALO * TLON, HEADS, HEAD)
        below_keys = lax.dynamic_slice(key_padded, (below_first, col_first, zero_index, zero_index), (HALO, TLON, HEADS, HEAD)).reshape(HALO * TLON, HEADS, HEAD)
        above_values = lax.dynamic_slice(value_padded, (row_first, col_first, zero_index, zero_index), (HALO, TLON, HEADS, HEAD)).reshape(HALO * TLON, HEADS, HEAD)
        below_values = lax.dynamic_slice(value_padded, (below_first, col_first, zero_index, zero_index), (HALO, TLON, HEADS, HEAD)).reshape(HALO * TLON, HEADS, HEAD)
        mask_row = mask_rows[tile_index]
        strip_allowed = jnp.broadcast_to((mask_row[column_band] > 0)[None, :], (TLAT, NLON)).reshape(TLAT * NLON)
        above_allowed = jnp.broadcast_to(strip_index > 0, (HALO * TLON,))
        below_allowed = jnp.broadcast_to(strip_index < N_LAT - 1, (HALO * TLON,))
        all_keys = jnp.concatenate([above_keys, below_keys, strip_keys], axis=0)
        all_values = jnp.concatenate([above_values, below_values, strip_values], axis=0)
        allowed = jnp.concatenate([above_allowed, below_allowed, strip_allowed], axis=0)
        scores = jnp.einsum('qhd,khd->hqk', query_tile.astype(jnp.float32), all_keys.astype(jnp.float32))
        scores = jnp.where(allowed[None, None, :], scores, MASKED)
        row_max = lax.optimization_barrier(jnp.max(scores, axis=-1))
        probs = jnp.where(allowed[None, None, :], jnp.exp(scores - row_max[..., None]), 0.0)
        summed = jnp.einsum('hqk,khd->hqd', probs.astype(jnp.bfloat16).astype(jnp.float32), all_values.astype(jnp.float32))
        context = summed / lax.optimization_barrier(jnp.sum(probs, axis=-1))[..., None]
        return jnp.transpose(context, (1, 0, 2)).reshape(TOKD, D).astype(jnp.bfloat16)
    contexts = lax.map(tile, jnp.arange(N_LAT * N_LON, dtype=jnp.int32))
    contexts = contexts.reshape(N_LAT, N_LON, TLAT, TLON, D)
    context = jnp.transpose(contexts, (0, 2, 1, 3, 4)).reshape(count_all, D)
    validity = patch_valid.reshape(count_all, 1).astype(jnp.float32)
    attended = jnp.dot(context, w_out, preferred_element_type=jnp.float32)
    hidden_state = (flattened + validity * attended).astype(jnp.bfloat16)
    residual = hidden_state.astype(jnp.float32)
    normed_two = layer_norm(residual, gain_mlp).astype(jnp.bfloat16)
    inner = jax.nn.gelu(jnp.dot(normed_two, w_up, preferred_element_type=jnp.float32)).astype(jnp.bfloat16)
    mixed = residual + validity * jnp.dot(inner, w_down, preferred_element_type=jnp.float32)
    return mixed.astype(jnp.bfloat16).reshape(NLAT, NLON, D)
```

```python
import functools

import jax
import jax.numpy as jnp
from jax import lax
from jax.experimental import pallas as pl
from jax.experimental.pallas import tpu as pltpu
from jax.sharding import Mesh, PartitionSpec as P

D = 768
HEADS = 12
HEAD = 64
FFW = 1536
TOK = 128
STRIPES = 16
LANES = 128
EDGE = 32
WIDE = 256
MASKED = -1e30
LON = ("y", "xl", "c")
CHIPS = ("y", "xl")
LAT = ("xh", "z")
BF = jnp.bfloat16
F32 = jnp.float32
VMEM_BYTES = 56 << 20


def norm_rows(x, gain):
    centre = jnp.mean(x, axis=-1, keepdims=True)
    diff = x - centre
    spread = jnp.mean(diff * diff, axis=-1, keepdims=True)
    return diff * lax.rsqrt(spread + 1e-05) * gain


def params():
    return pltpu.CompilerParams(vmem_limit_bytes=VMEM_BYTES)


def whole():
    return pl.BlockSpec(memory_space=pltpu.VMEM)


def scalar():
    return pl.BlockSpec(memory_space=pltpu.SMEM)


def cut_weights(place, qkv_ref, out_ref, up_ref, down_ref, piece_out):
    place_j = place[0]
    head = lax.rem(place_j, HEADS)
    block = head // 2
    odd = lax.rem(head, 2) == 1
    parts = []
    for which in range(3):
        start = pl.multiple_of(which * D + block * LANES, LANES)
        pair = qkv_ref[:, pl.ds(start, LANES)].astype(F32)
        parts.append(jnp.where(odd, pltpu.roll(pair, HEAD, 1), pair))
    low = lax.broadcasted_iota(jnp.int32, (24, LANES), 1) < HEAD
    piece_out[pl.ds(0, 24), :] = jnp.where(low, parts[0], pltpu.roll(parts[1], HEAD, 1)).astype(BF)
    piece_out[pl.ds(24, 24), :] = jnp.where(low, parts[2], 0.0).astype(BF)

    def fill(top, bottom):
        piece_out[pl.ds(48, 24), :] = top
        piece_out[pl.ds(72, 24), :] = bottom

    @pl.when(place_j < 6)
    def _():
        span = pl.ds(pl.multiple_of(place_j * LANES, LANES), LANES)
        fill(down_ref[pl.ds(0, 24), span], down_ref[pl.ds(24, 24), span])

    @pl.when((place_j >= 6) & (place_j < 9))
    def _():
        start = pl.multiple_of((place_j - 6) * 2 * LANES, LANES)
        fill(out_ref[:, pl.ds(start, LANES)], out_ref[:, pl.ds(start + LANES, LANES)])

    @pl.when(place_j >= 9)
    def _():
        start = pl.multiple_of(jnp.minimum(place_j - 9, 5) * 2 * LANES, LANES)
        fill(up_ref[:, pl.ds(start, LANES)], up_ref[:, pl.ds(start + LANES, LANES)])


def sort_mlp(place, rows_ref, mlp_out):
    place_j = place[0]

    @pl.when(place_j < 6)
    def _():
        for part in range(32):
            source = rows_ref.at[part % 16, (part // 16) ^ place[4]]
            mlp_out[pl.ds(part * 48, 48), :] = source[pl.ds(48, 48), :]

    @pl.when(place_j >= 6)
    def _():
        for part in range(32):
            source = rows_ref.at[part % 16, (part // 16) ^ place[4]]
            mlp_out[pl.ds(part * 24, 24), :] = source[pl.ds(48, 24), :]
            mlp_out[pl.ds(D + part * 24, 24), :] = source[pl.ds(72, 24), :]


def sort_head(place, rows_ref, head_out):
    for part in range(32):
        source = rows_ref.at[part % 16, (part // 16) ^ place[4]]
        head_out[pl.ds(part * 24, 24), pl.ds(0, LANES)] = source[pl.ds(0, 24), :]
        head_out[pl.ds(part * 24, 24), pl.ds(LANES, LANES)] = source[pl.ds(24, 24), :]


def first_norm(tokens_ref, gain_ref, mask_ref, spread_out):
    normed = norm_rows(tokens_ref[...].astype(F32), gain_ref[...].reshape(1, D)).astype(BF)
    seen = jnp.broadcast_to(mask_ref[0].astype(F32), (8, STRIPES))
    extra = jnp.concatenate([seen, jnp.zeros((8, D - STRIPES), F32)], axis=1).astype(BF)
    for peer in range(8):
        spread_out[peer, pl.ds(0, TOK), :] = normed
        spread_out[peer, pl.ds(TOK, 8), :] = extra


def project(near_ref, far_ref, weight_ref, q_out, k_out, vt_out, up_out, down_out, bias_out):
    weight = weight_ref[...]
    tops = []
    ends = []
    for tile in range(STRIPES):
        ref = near_ref if tile < 8 else far_ref
        rows = ref[tile % 8, pl.ds(0, TOK), :]
        full = jnp.dot(rows, weight, preferred_element_type=F32)
        qk = full[:, :LANES]
        qk_t = jnp.transpose(qk)
        v_t = jnp.transpose(full[:, LANES:])[:HEAD]
        span = pl.ds(tile * TOK, TOK)
        q_out[:, span] = (qk_t[:HEAD] * HEAD ** (-0.5)).astype(BF)
        k_out[span, :] = qk[:, HEAD:].astype(BF)
        vt_out[:, span] = v_t.astype(BF)
        kv_t = jnp.concatenate([qk_t[HEAD:], v_t], axis=0)
        seen = jnp.broadcast_to(ref[tile % 8, pl.ds(TOK, 8), :LANES].astype(F32)[:1], (LANES, LANES))
        bias_out[:, span] = jnp.where(jnp.transpose(seen)[:STRIPES] > 0, 0.0, MASKED)
        tops.append(kv_t[:, :EDGE])
        ends.append(kv_t[:, TOK - EDGE :])
    for group in range(4):
        span = pl.ds(group * LANES, LANES)
        up_out[:, span] = jnp.concatenate(tops[group * 4 : group * 4 + 4], axis=1).astype(BF)
        down_out[:, span] = jnp.concatenate(ends[group * 4 : group * 4 + 4], axis=1).astype(BF)


def attend_strip(
    place, q_ref, k_ref, vt_ref, bias_ref, acc_out, max_out, sum_out, even_scores, odd_scores, even_top, odd_top
):
    def score_chunk(group, chunk, scores, top):
        span = pl.ds(pl.multiple_of(group * WIDE, WIDE), WIDE)
        part = jnp.dot(k_ref[pl.ds(chunk * WIDE, WIDE), :], q_ref[:, span], preferred_element_type=F32)
        for half in range(2):
            tile = chunk * 2 + half
            side = place[3] if tile < 8 else 1 - place[3]
            row = bias_ref[pl.ds(2 * (tile % 8) + side, 1), span]
            piece = part[half * TOK : (half + 1) * TOK] + row
            scores[chunk, pl.ds(half * TOK, TOK), :] = piece
            best = jnp.max(piece.reshape(16, 8, WIDE), axis=0)
            top = best if top is None else jnp.maximum(top, best)
        return top

    def step(group, scores, top_ref, coming, next_scores, next_top):
        peak = jnp.max(top_ref[...], axis=0, keepdims=True)
        total = jnp.zeros((8, WIDE), F32)
        acc = jnp.zeros((HEAD, WIDE), F32)
        top = None
        for chunk in range(8):
            top = score_chunk(coming, chunk, next_scores, top)
            weights = jnp.exp(scores[chunk] - peak)
            total = total + jnp.sum(weights.reshape(32, 8, WIDE), axis=0)
            acc = acc + jnp.dot(
                vt_ref[:, pl.ds(chunk * WIDE, WIDE)], weights.astype(BF), preferred_element_type=F32
            )
        next_top[...] = top
        span = pl.ds(pl.multiple_of(group * WIDE, WIDE), WIDE)
        acc_out[:, span] = acc
        max_out[:, span] = jnp.broadcast_to(peak, (8, WIDE))
        sum_out[:, span] = jnp.broadcast_to(jnp.sum(total, axis=0, keepdims=True), (8, WIDE))

    top = None
    for chunk in range(8):
        top = score_chunk(0, chunk, even_scores, top)
    even_top[...] = top

    def pair(index, carry):
        first = index * 2
        step(first, even_scores, even_top, first + 1, odd_scores, odd_top)
        step(first + 1, odd_scores, odd_top, jnp.minimum(first + 2, 7), even_scores, even_top)
        return carry

    lax.fori_loop(0, 4, pair, 0)


def attend_edges(place, q_ref, above_ref, below_ref, acc_ref, max_ref, sum_ref, out_ref):
    core = place[3]
    key_band = lax.broadcasted_iota(jnp.int32, (LANES, 4 * TOK), 0) // EDGE
    query_band = lax.broadcasted_iota(jnp.int32, (LANES, 4 * TOK), 1) // TOK
    same = key_band == query_band
    for group in range(4):
        wide = slice(group * 4 * TOK, (group + 1) * 4 * TOK)
        keys = slice(group * LANES, (group + 1) * LANES)
        queries = q_ref[:, wide]
        scores = []
        for ref, flag in ((above_ref, place[1]), (below_ref, place[2])):
            part = lax.dot_general(
                ref[:HEAD, keys], queries, (((0,), (0,)), ((), ())), preferred_element_type=F32
            )
            scores.append(jnp.where(same & (flag > 0), part, MASKED))
        old = max_ref[:1, wide]
        peak = jnp.maximum(old, jnp.max(jnp.maximum(scores[0], scores[1]), axis=0, keepdims=True))
        factor = jnp.exp(old - peak)
        acc = acc_ref[:, wide] * factor
        total = sum_ref[:1, wide] * factor
        for ref, part in ((above_ref, scores[0]), (below_ref, scores[1])):
            weights = jnp.exp(part - peak)
            total = total + jnp.sum(weights, axis=0, keepdims=True)
            acc = acc + jnp.dot(ref[HEAD:, keys], weights.astype(BF), preferred_element_type=F32)
        result = (acc / total).astype(BF)
        for index in range(4):
            tile = group * 4 + index
            side = core if tile < 8 else 1 - core
            out_ref[2 * (tile % 8) + side] = result[:, index * TOK : (index + 1) * TOK]


def finish(ctx_ref, weights_hbm, tokens_ref, valid_ref, gain_ref, out_ref, w_out, w_up, w_down, sems):
    base = 6 * FFW
    jobs = [(w_out, unit, base + unit * D, D) for unit in range(6)]
    jobs += [(w_up, unit, base + (6 + unit) * D, D) for unit in range(12)]
    jobs += [(w_down, unit, unit * FFW, FFW) for unit in range(6)]
    copies = []
    for index, (target, unit, start, size) in enumerate(jobs):
        copy = pltpu.make_async_copy(
            weights_hbm.at[pl.ds(start, size), :], target.at[:, pl.ds(unit * LANES, LANES)], sems.at[index]
        )
        copy.start()
        copies.append(copy)
    context_t = ctx_ref[pl.ds(0, HEADS)].reshape(D, TOK)
    context = jnp.transpose(context_t.astype(F32)).astype(BF)
    valid = valid_ref[...].astype(F32)

    def wide_dot(rows, weight, chunk, first):
        copies[first + 2 * chunk].wait()
        copies[first + 2 * chunk + 1].wait()
        return jnp.dot(rows, weight[:, pl.ds(chunk * WIDE, WIDE)], preferred_element_type=F32)

    attended = jnp.concatenate([wide_dot(context, w_out, chunk, 0) for chunk in range(3)], axis=1)
    hidden = (tokens_ref[...].astype(F32) + valid * attended).astype(BF)
    residual = hidden.astype(F32)
    normed = norm_rows(residual, gain_ref[...].reshape(1, D)).astype(BF)
    inner = jnp.concatenate(
        [jax.nn.gelu(wide_dot(normed, w_up, chunk, 6)).astype(BF) for chunk in range(6)], axis=1
    )
    for chunk in range(3):
        down = wide_dot(inner, w_down, chunk, 18)
        span = slice(chunk * WIDE, (chunk + 1) * WIDE)
        out_ref[:, span] = (residual[:, span] + valid * down).astype(BF)


def body(tokens, patch_valid, block_mask, gain_attn, gain_mlp, w_qkv, w_out, w_up, w_down):
    lat_rows, lon_cols = tokens.shape[0], tokens.shape[1]
    place_j = lax.axis_index(LON)
    core = lax.axis_index("c")
    place_i = lax.axis_index(LAT)
    place = jnp.stack(
        [
            place_j,
            (place_i > 0).astype(jnp.int32),
            (place_i < 31).astype(jnp.int32),
            core,
            lax.axis_index("xh"),
        ]
    ).astype(jnp.int32)
    own = tokens.reshape(TOK, D)
    piece = pl.pallas_call(
        cut_weights,
        out_shape=jax.ShapeDtypeStruct((96, LANES), BF),
        in_specs=[scalar()] + [whole()] * 4,
        out_specs=whole(),
        compiler_params=params(),
        name="cut_weights",
    )(place, w_qkv, w_out, w_up, w_down)
    twin = lax.ppermute(piece, "xh", [(0, 1), (1, 0)])
    own, piece = lax.optimization_barrier((own, piece))
    spread = pl.pallas_call(
        first_norm,
        out_shape=jax.ShapeDtypeStruct((8, TOK + 8, D), BF),
        in_specs=[whole()] * 3,
        out_specs=whole(),
        compiler_params=params(),
        name="first_norm",
    )(own, gain_attn, block_mask)
    both = jnp.stack([piece, twin])
    both, spread = lax.optimization_barrier((both, spread))
    near = lax.all_to_all(spread, CHIPS, 0, 0)
    rows = lax.all_gather(both, "z", axis=0)
    near, rows = lax.optimization_barrier((near, rows))
    far = lax.ppermute(near, "c", [(0, 1), (1, 0)])
    mlp_rows = pl.pallas_call(
        sort_mlp,
        out_shape=jax.ShapeDtypeStruct((FFW, LANES), BF),
        in_specs=[scalar(), whole()],
        out_specs=whole(),
        compiler_params=params(),
        name="sort_mlp",
    )(place, rows)
    head_w = pl.pallas_call(
        sort_head,
        out_shape=jax.ShapeDtypeStruct((D, 2 * LANES), BF),
        in_specs=[scalar(), whole()],
        out_specs=whole(),
        compiler_params=params(),
        name="sort_head",
    )(place, rows)
    mlp_all = lax.all_gather(mlp_rows, LON, axis=0, tiled=True)

    halo = jax.ShapeDtypeStruct((LANES, 4 * LANES), BF)
    keys = STRIPES * TOK
    q_t, k_n, v_t, to_up, to_down, bias = pl.pallas_call(
        project,
        out_shape=(
            jax.ShapeDtypeStruct((HEAD, keys), BF),
            jax.ShapeDtypeStruct((keys, HEAD), BF),
            jax.ShapeDtypeStruct((HEAD, keys), BF),
            halo,
            halo,
            jax.ShapeDtypeStruct((STRIPES, keys), F32),
        ),
        in_specs=[whole()] * 3,
        out_specs=(whole(),) * 6,
        compiler_params=params(),
        cost_estimate=pl.CostEstimate(flops=2 * 2048 * 768 * 256, bytes_accessed=5 << 20, transcendentals=0),
        name="project",
    )(near, far, head_w)
    above = lax.ppermute(to_down, LAT, [(i, i + 1) for i in range(31)])
    below = lax.ppermute(to_up, LAT, [(i + 1, i) for i in range(31)])

    stat = jax.ShapeDtypeStruct((8, keys), F32)
    acc, peaks, sums = pl.pallas_call(
        attend_strip,
        out_shape=(jax.ShapeDtypeStruct((HEAD, keys), F32), stat, stat),
        in_specs=[scalar()] + [whole()] * 4,
        out_specs=(whole(),) * 3,
        scratch_shapes=[
            pltpu.VMEM((8, WIDE, WIDE), F32),
            pltpu.VMEM((8, WIDE, WIDE), F32),
            pltpu.VMEM((8, WIDE), F32),
            pltpu.VMEM((8, WIDE), F32),
        ],
        compiler_params=params(),
        cost_estimate=pl.CostEstimate(
            flops=4 * 2048 * 2048 * 256, bytes_accessed=3 << 20, transcendentals=2048 * 2048
        ),
        name="attend_strip",
    )(place, q_t, k_n, v_t, bias)

    context = pl.pallas_call(
        attend_edges,
        out_shape=jax.ShapeDtypeStruct((STRIPES, HEAD, TOK), BF),
        in_specs=[scalar()] + [whole()] * 6,
        out_specs=whole(),
        compiler_params=params(),
        name="attend_edges",
    )(place, q_t, above, below, acc, peaks, sums)

    mine = lax.all_to_all(context, LON, 0, 0)
    mixed = pl.pallas_call(
        finish,
        out_shape=jax.ShapeDtypeStruct((TOK, D), BF),
        in_specs=[whole(), pl.BlockSpec(memory_space=pl.ANY)] + [whole()] * 3,
        out_specs=whole(),
        scratch_shapes=[
            pltpu.VMEM((D, D), BF),
            pltpu.VMEM((D, FFW), BF),
            pltpu.VMEM((FFW, D), BF),
            pltpu.SemaphoreType.DMA((24,)),
        ],
        compiler_params=params(),
        cost_estimate=pl.CostEstimate(flops=2 * 128 * 768 * 3840, bytes_accessed=7 << 20, transcendentals=128 * 1536),
        name="finish",
    )(mine, mlp_all, own, patch_valid.reshape(TOK, 1), gain_mlp)
    return mixed.reshape(lat_rows, lon_cols, D)


def solution(mesh):
    fine = Mesh(mesh.devices.reshape(4, 2, 2, 2, 16), ("y", "xl", "c", "xh", "z"))
    in_specs = (
        P(LAT, LON, None),
        P(LAT, LON),
        P(LAT, LON, None),
        P(),
        P(),
        P(LAT, None),
        P(LAT, None),
        P(LAT, None),
        P(LAT, None),
    )
    out_specs = P(LAT, LON, None)
    return jax.shard_map(body, mesh=fine, in_specs=in_specs, out_specs=out_specs, check_vma=False)
```

```python
import functools

import jax
import jax.numpy as jnp
from jax import lax
from jax.experimental import pallas as pl
from jax.experimental.pallas import tpu as pltpu
from jax.sharding import Mesh, PartitionSpec as P

D = 768
HEADS = 12
HEAD = 64
FFW = 1536
TOK = 128
STRIPES = 16
LANES = 128
EDGE = 32
WIDE = 256
MASKED = -1e30
LON = ("y", "xl", "c")
CHIPS = ("y", "xl")
LAT = ("xh", "z")
BF = jnp.bfloat16
F32 = jnp.float32
VMEM_BYTES = 56 << 20


def norm_rows(x, gain):
    centre = jnp.mean(x, axis=-1, keepdims=True)
    diff = x - centre
    spread = jnp.mean(diff * diff, axis=-1, keepdims=True)
    return diff * lax.rsqrt(spread + 1e-05) * gain


def params():
    return pltpu.CompilerParams(vmem_limit_bytes=VMEM_BYTES)


def whole():
    return pl.BlockSpec(memory_space=pltpu.VMEM)


def scalar():
    return pl.BlockSpec(memory_space=pltpu.SMEM)


def first_norm(tokens_ref, gain_ref, mask_ref, norm_out):
    norm_out[pl.ds(0, TOK), :] = norm_rows(
        tokens_ref[...].astype(F32), gain_ref[...].reshape(1, D)
    ).astype(BF)
    seen = jnp.broadcast_to(mask_ref[0].astype(F32), (8, STRIPES))
    norm_out[pl.ds(TOK, 8), :] = jnp.concatenate([seen, jnp.zeros((8, D - STRIPES), F32)], axis=1).astype(BF)


def cut_weights(place, qkv_ref, out_ref, up_ref, down_ref, order_ref, piece_out):
    place_j = place[0]
    head = lax.rem(place_j, HEADS)
    block = head // 2
    odd = lax.rem(head, 2) == 1
    parts = []
    for which in range(3):
        start = pl.multiple_of(which * D + block * LANES, LANES)
        pair = qkv_ref[:, pl.ds(start, LANES)].astype(F32)
        parts.append(jnp.where(odd, pltpu.roll(pair, HEAD, 1), pair))
    low = lax.broadcasted_iota(jnp.int32, (24, LANES), 1) < HEAD
    qk = jnp.where(low, parts[0], pltpu.roll(parts[1], HEAD, 1)).astype(BF)
    v = jnp.where(low, parts[2], 0.0).astype(BF)
    for peer in range(32):
        piece_out[peer, pl.ds(0, 24), :] = qk
        piece_out[peer, pl.ds(24, 24), :] = v

    def fill(top, bottom):
        for peer in range(32):
            piece_out[peer, pl.ds(48, 24), :] = top
            piece_out[peer, pl.ds(72, 24), :] = bottom

    @pl.when(place_j < 6)
    def _():
        span = pl.ds(pl.multiple_of(place_j * LANES, LANES), LANES)
        fill(down_ref[pl.ds(0, 24), span], down_ref[pl.ds(24, 24), span])

    @pl.when((place_j >= 6) & (place_j < 9))
    def _():
        start = pl.multiple_of((place_j - 6) * 2 * LANES, LANES)
        fill(out_ref[:, pl.ds(start, LANES)], out_ref[:, pl.ds(start + LANES, LANES)])

    @pl.when(place_j >= 9)
    def _():
        start = pl.multiple_of(jnp.minimum(place_j - 9, 5) * 2 * LANES, LANES)
        fill(up_ref[:, pl.ds(start, LANES)], up_ref[:, pl.ds(start + LANES, LANES)])


def sort_mlp(place, rows_ref, mlp_out):
    place_j = place[0]

    @pl.when(place_j < 6)
    def _():
        for part in range(32):
            rows = rows_ref[part, pl.ds(48, 48), :]
            for peer in range(8):
                mlp_out[peer, pl.ds(part * 48, 48), :] = rows

    @pl.when(place_j >= 6)
    def _():
        for part in range(32):
            top = rows_ref[part, pl.ds(48, 24), :]
            bottom = rows_ref[part, pl.ds(72, 24), :]
            for peer in range(8):
                mlp_out[peer, pl.ds(part * 24, 24), :] = top
                mlp_out[peer, pl.ds(D + part * 24, 24), :] = bottom


def sort_head(rows_ref, head_out):
    for part in range(32):
        head_out[pl.ds(part * 24, 24), pl.ds(0, LANES)] = rows_ref[part, pl.ds(0, 24), :]
        head_out[pl.ds(part * 24, 24), pl.ds(LANES, LANES)] = rows_ref[part, pl.ds(24, 24), :]


def project(normed_ref, weight_ref, q_out, k_out, vt_out, up_out, down_out, bias_out):
    weight = weight_ref[...]
    tops = []
    ends = []
    for tile in range(4):
        full = jnp.dot(normed_ref[tile, pl.ds(0, TOK), :], weight, preferred_element_type=F32)
        qk = full[:, :LANES]
        qk_t = jnp.transpose(qk)
        v_t = jnp.transpose(full[:, LANES:])[:HEAD]
        span = pl.ds(tile * TOK, TOK)
        q_out[:, span] = (qk_t[:HEAD] * HEAD ** (-0.5)).astype(BF)
        k_out[span, :] = qk[:, HEAD:].astype(BF)
        vt_out[:, span] = v_t.astype(BF)
        kv_t = jnp.concatenate([qk_t[HEAD:], v_t], axis=0)
        seen = jnp.broadcast_to(normed_ref[tile, pl.ds(TOK, 8), :LANES].astype(F32)[:1], (LANES, LANES))
        bias_out[:, span] = jnp.where(jnp.transpose(seen)[:STRIPES] > 0, 0.0, MASKED)
        tops.append(kv_t[:, :EDGE])
        ends.append(kv_t[:, TOK - EDGE :])
    up_out[...] = jnp.concatenate(tops, axis=1).astype(BF)
    down_out[...] = jnp.concatenate(ends, axis=1).astype(BF)


def attend_strip(
    q_ref, k_ref, vt_ref, bias_ref, acc_out, max_out, sum_out, even_scores, odd_scores, even_top, odd_top
):
    def score_chunk(group, chunk, scores, top):
        span = pl.ds(pl.multiple_of(group * WIDE, WIDE), WIDE)
        part = jnp.dot(k_ref[pl.ds(chunk * WIDE, WIDE), :], q_ref[:, span], preferred_element_type=F32)
        for half in range(2):
            row = bias_ref[pl.ds(chunk * 2 + half, 1), span]
            piece = part[half * TOK : (half + 1) * TOK] + row
            scores[chunk, pl.ds(half * TOK, TOK), :] = piece
            best = jnp.max(piece.reshape(16, 8, WIDE), axis=0)
            top = best if top is None else jnp.maximum(top, best)
        return top

    def step(group, scores, top_ref, coming, next_scores, next_top):
        peak = jnp.max(top_ref[...], axis=0, keepdims=True)
        total = jnp.zeros((8, WIDE), F32)
        acc = jnp.zeros((HEAD, WIDE), F32)
        top = None
        for chunk in range(8):
            top = score_chunk(coming, chunk, next_scores, top)
            weights = jnp.exp(scores[chunk] - peak)
            total = total + jnp.sum(weights.reshape(32, 8, WIDE), axis=0)
            acc = acc + jnp.dot(
                vt_ref[:, pl.ds(chunk * WIDE, WIDE)], weights.astype(BF), preferred_element_type=F32
            )
        next_top[...] = top
        span = pl.ds(pl.multiple_of(group * WIDE, WIDE), WIDE)
        acc_out[:, span] = acc
        max_out[:, span] = jnp.broadcast_to(peak, (8, WIDE))
        sum_out[:, span] = jnp.broadcast_to(jnp.sum(total, axis=0, keepdims=True), (8, WIDE))

    top = None
    for chunk in range(8):
        top = score_chunk(0, chunk, even_scores, top)
    even_top[...] = top

    def pair(index, carry):
        first = index * 2
        step(first, even_scores, even_top, first + 1, odd_scores, odd_top)
        step(first + 1, odd_scores, odd_top, jnp.minimum(first + 2, 7), even_scores, even_top)
        return carry

    lax.fori_loop(0, 4, pair, 0)


def attend_edges(place, q_ref, above_ref, below_ref, acc_ref, max_ref, sum_ref, out_ref):
    key_band = lax.broadcasted_iota(jnp.int32, (LANES, 4 * TOK), 0) // EDGE
    query_band = lax.broadcasted_iota(jnp.int32, (LANES, 4 * TOK), 1) // TOK
    same = key_band == query_band
    for group in range(4):
        wide = slice(group * 4 * TOK, (group + 1) * 4 * TOK)
        keys = slice(group * LANES, (group + 1) * LANES)
        queries = q_ref[:, wide]
        scores = []
        for ref, flag in ((above_ref, place[1]), (below_ref, place[2])):
            part = lax.dot_general(
                ref[:HEAD, keys], queries, (((0,), (0,)), ((), ())), preferred_element_type=F32
            )
            scores.append(jnp.where(same & (flag > 0), part, MASKED))
        old = max_ref[:1, wide]
        peak = jnp.maximum(old, jnp.max(jnp.maximum(scores[0], scores[1]), axis=0, keepdims=True))
        factor = jnp.exp(old - peak)
        acc = acc_ref[:, wide] * factor
        total = sum_ref[:1, wide] * factor
        for ref, part in ((above_ref, scores[0]), (below_ref, scores[1])):
            weights = jnp.exp(part - peak)
            total = total + jnp.sum(weights, axis=0, keepdims=True)
            acc = acc + jnp.dot(ref[HEAD:, keys], weights.astype(BF), preferred_element_type=F32)
        result = (acc / total).astype(BF)
        for index in range(4):
            out_ref[group * 4 + index] = result[:, index * TOK : (index + 1) * TOK]


def finish(
    place, ctx_ref, near_hbm, far_hbm, tokens_ref, valid_ref, gain_ref, out_ref, w_in, w_down, sems
):
    core = place[3]

    def start(source, chip, side):
        part = 2 * chip + side
        if chip < 3:
            pltpu.make_async_copy(
                source.at[chip],
                w_down.at[:, pl.ds(pl.multiple_of(part * LANES, LANES), LANES)],
                sems.at[2 * part],
            ).start()
        else:
            for half in range(2):
                unit = 2 * (part - 6) + half
                pltpu.make_async_copy(
                    source.at[chip, pl.ds(half * D, D), :],
                    w_in.at[:, pl.ds(pl.multiple_of(unit * LANES, LANES), LANES)],
                    sems.at[2 * part + half],
                ).start()

    for chip in (3, 4, 5, 6, 7, 0, 1, 2):
        start(near_hbm, chip, core)
        start(far_hbm, chip, 1 - core)

    def settle(part):
        if part < 6:
            pltpu.make_async_copy(
                near_hbm.at[0], w_down.at[:, pl.ds(part * LANES, LANES)], sems.at[2 * part]
            ).wait()
        else:
            for half in range(2):
                unit = 2 * (part - 6) + half
                pltpu.make_async_copy(
                    near_hbm.at[0, pl.ds(0, D), :],
                    w_in.at[:, pl.ds(unit * LANES, LANES)],
                    sems.at[2 * part + half],
                ).wait()

    context_t = ctx_ref[pl.ds(0, HEADS)].reshape(D, TOK)
    context = jnp.transpose(context_t.astype(F32)).astype(BF)
    valid = valid_ref[...].astype(F32)

    def into(rows, part):
        settle(part)
        return jnp.dot(rows, w_in[:, pl.ds((part - 6) * WIDE, WIDE)], preferred_element_type=F32)

    attended = jnp.concatenate([into(context, part) for part in range(6, 9)], axis=1)
    hidden = (tokens_ref[...].astype(F32) + valid * attended).astype(BF)
    residual = hidden.astype(F32)
    normed = norm_rows(residual, gain_ref[...].reshape(1, D)).astype(BF)
    inner = jnp.concatenate([jax.nn.gelu(into(normed, part)).astype(BF) for part in range(9, 15)], axis=1)
    settle(15)
    for chunk in range(3):
        settle(2 * chunk)
        settle(2 * chunk + 1)
        span = slice(chunk * WIDE, (chunk + 1) * WIDE)
        down = jnp.dot(inner, w_down[:, span], preferred_element_type=F32)
        out_ref[:, span] = (residual[:, span] + valid * down).astype(BF)


def body(tokens, patch_valid, block_mask, gain_attn, gain_mlp, w_qkv, w_out, w_up, w_down):
    lat_rows, lon_cols = tokens.shape[0], tokens.shape[1]
    place_j = lax.axis_index(LON)
    core = lax.axis_index("c")
    place_i = lax.axis_index(LAT)
    place = jnp.stack(
        [
            place_j,
            (place_i > 0).astype(jnp.int32),
            (place_i < 31).astype(jnp.int32),
            core,
        ]
    ).astype(jnp.int32)
    own = tokens.reshape(TOK, D)
    normed = pl.pallas_call(
        first_norm,
        out_shape=jax.ShapeDtypeStruct((TOK + 8, D), BF),
        in_specs=[whole()] * 3,
        out_specs=whole(),
        compiler_params=params(),
        name="first_norm",
    )(own, gain_attn, block_mask)
    piece = pl.pallas_call(
        cut_weights,
        out_shape=jax.ShapeDtypeStruct((32, 96, LANES), BF),
        in_specs=[scalar()] + [whole()] * 4 + [pl.BlockSpec(memory_space=pl.ANY)],
        out_specs=whole(),
        compiler_params=params(),
        name="cut_weights",
    )(place, w_qkv, w_out, w_up, w_down, normed)
    strip = lax.all_gather(normed, LON, axis=0)
    rows = lax.all_to_all(piece, LAT, 0, 0)
    mlp_rows = pl.pallas_call(
        sort_mlp,
        out_shape=jax.ShapeDtypeStruct((8, FFW, LANES), BF),
        in_specs=[scalar(), whole()],
        out_specs=whole(),
        compiler_params=params(),
        name="sort_mlp",
    )(place, rows)
    near = lax.all_to_all(mlp_rows, CHIPS, 0, 0)
    head_w = pl.pallas_call(
        sort_head,
        out_shape=jax.ShapeDtypeStruct((D, 2 * LANES), BF),
        in_specs=[whole()],
        out_specs=whole(),
        compiler_params=params(),
        name="sort_head",
    )(rows)
    halo = jax.ShapeDtypeStruct((LANES, 4 * LANES), BF)
    keys = STRIPES * TOK
    q_t, k_n, v_t, to_up, to_down, bias = pl.pallas_call(
        project,
        out_shape=(
            jax.ShapeDtypeStruct((HEAD, keys), BF),
            jax.ShapeDtypeStruct((keys, HEAD), BF),
            jax.ShapeDtypeStruct((HEAD, keys), BF),
            halo,
            halo,
            jax.ShapeDtypeStruct((STRIPES, keys), F32),
        ),
        grid=(4,),
        in_specs=[
            pl.BlockSpec((4, TOK + 8, D), lambda g: (g, 0, 0)),
            pl.BlockSpec((D, 2 * LANES), lambda g: (0, 0)),
        ],
        out_specs=(
            pl.BlockSpec((HEAD, 4 * TOK), lambda g: (0, g)),
            pl.BlockSpec((4 * TOK, HEAD), lambda g: (g, 0)),
            pl.BlockSpec((HEAD, 4 * TOK), lambda g: (0, g)),
            pl.BlockSpec((LANES, LANES), lambda g: (0, g)),
            pl.BlockSpec((LANES, LANES), lambda g: (0, g)),
            pl.BlockSpec((STRIPES, 4 * TOK), lambda g: (0, g)),
        ),
        compiler_params=params(),
        cost_estimate=pl.CostEstimate(flops=2 * 2048 * 768 * 256, bytes_accessed=5 << 20, transcendentals=0),
        name="project",
    )(strip, head_w)
    above = lax.ppermute(to_down, LAT, [(i, i + 1) for i in range(31)])
    below = lax.ppermute(to_up, LAT, [(i + 1, i) for i in range(31)])

    stat = jax.ShapeDtypeStruct((8, keys), F32)
    acc, peaks, sums = pl.pallas_call(
        attend_strip,
        out_shape=(jax.ShapeDtypeStruct((HEAD, keys), F32), stat, stat),
        in_specs=[whole()] * 4,
        out_specs=(whole(),) * 3,
        scratch_shapes=[
            pltpu.VMEM((8, WIDE, WIDE), F32),
            pltpu.VMEM((8, WIDE, WIDE), F32),
            pltpu.VMEM((8, WIDE), F32),
            pltpu.VMEM((8, WIDE), F32),
        ],
        compiler_params=params(),
        cost_estimate=pl.CostEstimate(
            flops=4 * 2048 * 2048 * 256, bytes_accessed=3 << 20, transcendentals=2048 * 2048
        ),
        name="attend_strip",
    )(q_t, k_n, v_t, bias)

    context = pl.pallas_call(
        attend_edges,
        out_shape=jax.ShapeDtypeStruct((STRIPES, HEAD, TOK), BF),
        in_specs=[scalar()] + [whole()] * 6,
        out_specs=whole(),
        compiler_params=params(),
        name="attend_edges",
    )(place, q_t, above, below, acc, peaks, sums)

    near, context = lax.optimization_barrier((near, context))
    far = lax.ppermute(near, "c", [(0, 1), (1, 0)])
    mine = lax.all_to_all(context, LON, 0, 0)
    mixed = pl.pallas_call(
        finish,
        out_shape=jax.ShapeDtypeStruct((TOK, D), BF),
        in_specs=[scalar(), whole()] + [pl.BlockSpec(memory_space=pl.ANY)] * 2 + [whole()] * 3,
        out_specs=whole(),
        scratch_shapes=[
            pltpu.VMEM((D, 20 * LANES), BF),
            pltpu.VMEM((FFW, D), BF),
            pltpu.SemaphoreType.DMA((32,)),
        ],
        compiler_params=params(),
        cost_estimate=pl.CostEstimate(flops=2 * 128 * 768 * 3840, bytes_accessed=7 << 20, transcendentals=128 * 1536),
        name="finish",
    )(place, mine, near, far, own, patch_valid.reshape(TOK, 1), gain_mlp)
    return mixed.reshape(lat_rows, lon_cols, D)


def solution(mesh):
    fine = Mesh(mesh.devices.reshape(4, 2, 2, 2, 16), ("y", "xl", "c", "xh", "z"))
    in_specs = (
        P(LAT, LON, None),
        P(LAT, LON),
        P(LAT, LON, None),
        P(),
        P(),
        P(LAT, None),
        P(LAT, None),
        P(LAT, None),
        P(LAT, None),
    )
    out_specs = P(LAT, LON, None)
    return jax.shard_map(body, mesh=fine, in_specs=in_specs, out_specs=out_specs, check_vma=False)
```

```python
import functools

import jax
import jax.numpy as jnp
from jax import lax
from jax.experimental import pallas as pl
from jax.experimental.pallas import tpu as pltpu
from jax.sharding import Mesh, PartitionSpec as P

D = 768
HEADS = 12
HEAD = 64
FFW = 1536
TOK = 128
STRIPES = 16
LANES = 128
EDGE = 32
WIDE = 256
MASKED = -1e30
LON = ("y", "xl", "c")
PLANE = ("xh", "y", "xl")
LAT = ("xh", "z")
BF = jnp.bfloat16
F32 = jnp.float32


def norm_rows(x, gain):
    centre = jnp.mean(x, axis=-1, keepdims=True)
    diff = x - centre
    spread = jnp.mean(diff * diff, axis=-1, keepdims=True)
    return diff * lax.rsqrt(spread + 1e-05) * gain


def params(mib):
    return pltpu.CompilerParams(vmem_limit_bytes=mib << 20)


def whole():
    return pl.BlockSpec(memory_space=pltpu.VMEM)


def prepare(tokens_ref, gain_ref, mask_ref, qkv_ref, out_ref, up_ref, down_ref, norm_out, piece_out):
    norm_out[pl.ds(0, TOK), :] = norm_rows(
        tokens_ref[...].astype(F32), gain_ref[...].reshape(1, D)
    ).astype(BF)
    seen = jnp.broadcast_to(mask_ref[0].astype(F32), (8, STRIPES))
    norm_out[pl.ds(TOK, 8), :] = jnp.concatenate([seen, jnp.zeros((8, D - STRIPES), F32)], axis=1).astype(BF)

    place_j = (lax.axis_index("y") * 2 + lax.axis_index("xl")) * 2 + lax.axis_index("c")
    head = lax.rem(place_j, HEADS)
    block = head // 2
    odd = lax.rem(head, 2) == 1
    parts = []
    for which in range(3):
        start = pl.multiple_of(which * D + block * LANES, LANES)
        pair = qkv_ref[:, pl.ds(start, LANES)].astype(F32)
        parts.append(jnp.where(odd, pltpu.roll(pair, HEAD, 1), pair))
    low = lax.broadcasted_iota(jnp.int32, (24, LANES), 1) < HEAD
    qk = jnp.where(low, parts[0], pltpu.roll(parts[1], HEAD, 1)).astype(BF)
    v = jnp.where(low, parts[2], 0.0).astype(BF)
    piece_out[pl.ds(0, 24), :] = qk
    piece_out[pl.ds(24, 24), :] = v

    def fill(top, bottom):
        piece_out[pl.ds(48, 24), :] = top
        piece_out[pl.ds(72, 24), :] = bottom

    @pl.when(place_j < 6)
    def _():
        span = pl.ds(pl.multiple_of(place_j * LANES, LANES), LANES)
        fill(down_ref[pl.ds(0, 24), span], down_ref[pl.ds(24, 24), span])

    @pl.when((place_j >= 6) & (place_j < 9))
    def _():
        start = pl.multiple_of((place_j - 6) * 2 * LANES, LANES)
        fill(out_ref[:, pl.ds(start, LANES)], out_ref[:, pl.ds(start + LANES, LANES)])

    @pl.when(place_j >= 9)
    def _():
        start = pl.multiple_of(jnp.minimum(place_j - 9, 5) * 2 * LANES, LANES)
        fill(up_ref[:, pl.ds(start, LANES)], up_ref[:, pl.ds(start + LANES, LANES)])


def sort_rows(rows_ref, mlp_hbm, head_out, mlp_rows, sems):
    place_j = (lax.axis_index("y") * 2 + lax.axis_index("xl")) * 2 + lax.axis_index("c")

    @pl.when(place_j < 6)
    def _():
        for part in range(16):
            mlp_rows[pl.ds(part * 48, 48), :] = rows_ref[part, pl.ds(48, 48), :]

    @pl.when(place_j >= 6)
    def _():
        for part in range(16):
            mlp_rows[pl.ds(part * 24, 24), :] = rows_ref[part, pl.ds(48, 24), :]
            mlp_rows[pl.ds(D // 2 + part * 24, 24), :] = rows_ref[part, pl.ds(72, 24), :]

    copies = [pltpu.make_async_copy(mlp_rows, mlp_hbm.at[peer], sems.at[peer]) for peer in range(16)]
    for copy in copies:
        copy.start()
    for part in range(16):
        head_out[pl.ds(part * 24, 24), pl.ds(0, LANES)] = rows_ref[part, pl.ds(0, 24), :]
        head_out[pl.ds(part * 24, 24), pl.ds(LANES, LANES)] = rows_ref[part, pl.ds(24, 24), :]
    for copy in copies:
        copy.wait()


def project(normed_ref, mine_ref, twin_ref, q_out, k_out, vt_out, up_out, down_out, bias_out):
    lower = lax.axis_index("xh") == 0
    first = jnp.where(lower, mine_ref[...], twin_ref[...])
    last = jnp.where(lower, twin_ref[...], mine_ref[...])
    weight = jnp.concatenate([first, last], axis=0)
    tops = []
    ends = []
    for tile in range(STRIPES):
        full = jnp.dot(normed_ref[tile, pl.ds(0, TOK), :], weight, preferred_element_type=F32)
        qk = full[:, :LANES]
        qk_t = jnp.transpose(qk)
        v_t = jnp.transpose(full[:, LANES:])[:HEAD]
        span = pl.ds(tile * TOK, TOK)
        q_out[:, span] = (qk_t[:HEAD] * HEAD ** (-0.5)).astype(BF)
        k_out[span, :] = qk[:, HEAD:].astype(BF)
        vt_out[:, span] = v_t.astype(BF)
        kv_t = jnp.concatenate([qk_t[HEAD:], v_t], axis=0)
        seen = jnp.broadcast_to(normed_ref[tile, pl.ds(TOK, 8), :LANES].astype(F32)[:1], (LANES, LANES))
        bias_out[:, span] = jnp.where(jnp.transpose(seen)[:STRIPES] > 0, 0.0, MASKED)
        tops.append(kv_t[:, :EDGE])
        ends.append(kv_t[:, TOK - EDGE :])
    for group in range(4):
        span = pl.ds(group * LANES, LANES)
        up_out[:, span] = jnp.concatenate(tops[group * 4 : group * 4 + 4], axis=1).astype(BF)
        down_out[:, span] = jnp.concatenate(ends[group * 4 : group * 4 + 4], axis=1).astype(BF)


def attend_strip(
    q_ref, k_ref, vt_ref, bias_ref, acc_out, max_out, sum_out, even_scores, odd_scores, even_top, odd_top
):
    def score_chunk(group, chunk, scores, top):
        span = pl.ds(pl.multiple_of(group * WIDE, WIDE), WIDE)
        part = jnp.dot(k_ref[pl.ds(chunk * WIDE, WIDE), :], q_ref[:, span], preferred_element_type=F32)
        for half in range(2):
            row = bias_ref[pl.ds(chunk * 2 + half, 1), span]
            piece = part[half * TOK : (half + 1) * TOK] + row
            scores[chunk, pl.ds(half * TOK, TOK), :] = piece
            best = jnp.max(piece.reshape(16, 8, WIDE), axis=0)
            top = best if top is None else jnp.maximum(top, best)
        return top

    def step(group, scores, top_ref, coming, next_scores, next_top):
        peak = jnp.max(top_ref[...], axis=0, keepdims=True)
        total = jnp.zeros((8, WIDE), F32)
        acc = jnp.zeros((HEAD, WIDE), F32)
        top = None
        for chunk in range(8):
            top = score_chunk(coming, chunk, next_scores, top)
            weights = jnp.exp(scores[chunk] - peak)
            total = total + jnp.sum(weights.reshape(32, 8, WIDE), axis=0)
            acc = acc + jnp.dot(
                vt_ref[:, pl.ds(chunk * WIDE, WIDE)], weights.astype(BF), preferred_element_type=F32
            )
        next_top[...] = top
        span = pl.ds(pl.multiple_of(group * WIDE, WIDE), WIDE)
        acc_out[:, span] = acc
        max_out[:, span] = jnp.broadcast_to(peak, (8, WIDE))
        sum_out[:, span] = jnp.broadcast_to(jnp.sum(total, axis=0, keepdims=True), (8, WIDE))

    top = None
    for chunk in range(8):
        top = score_chunk(0, chunk, even_scores, top)
    even_top[...] = top

    def pair(index, carry):
        first = index * 2
        step(first, even_scores, even_top, first + 1, odd_scores, odd_top)
        step(first + 1, odd_scores, odd_top, jnp.minimum(first + 2, 7), even_scores, even_top)
        return carry

    lax.fori_loop(0, 4, pair, 0)


def attend_edges(q_ref, above_ref, below_ref, acc_ref, max_ref, sum_ref, out_ref):
    row = lax.axis_index("xh") * 16 + lax.axis_index("z")
    key_band = lax.broadcasted_iota(jnp.int32, (LANES, 4 * TOK), 0) // EDGE
    query_band = lax.broadcasted_iota(jnp.int32, (LANES, 4 * TOK), 1) // TOK
    same = key_band == query_band
    for group in range(4):
        wide = slice(group * 4 * TOK, (group + 1) * 4 * TOK)
        keys = slice(group * LANES, (group + 1) * LANES)
        queries = q_ref[:, wide]
        scores = []
        for ref, flag in ((above_ref, row > 0), (below_ref, row < 31)):
            part = lax.dot_general(
                ref[:HEAD, keys], queries, (((0,), (0,)), ((), ())), preferred_element_type=F32
            )
            scores.append(jnp.where(same & flag, part, MASKED))
        old = max_ref[:1, wide]
        peak = jnp.maximum(old, jnp.max(jnp.maximum(scores[0], scores[1]), axis=0, keepdims=True))
        factor = jnp.exp(old - peak)
        acc = acc_ref[:, wide] * factor
        total = sum_ref[:1, wide] * factor
        for ref, part in ((above_ref, scores[0]), (below_ref, scores[1])):
            weights = jnp.exp(part - peak)
            total = total + jnp.sum(weights, axis=0, keepdims=True)
            acc = acc + jnp.dot(ref[HEAD:, keys], weights.astype(BF), preferred_element_type=F32)
        result = (acc / total).astype(BF)
        for index in range(4):
            out_ref[group * 4 + index] = result[:, index * TOK : (index + 1) * TOK]


def finish(ctx_ref, near_ref, far_ref, tokens_ref, valid_ref, gain_ref, out_ref):
    core = lax.axis_index("c")

    def run(even_ref, odd_ref):
        context_t = ctx_ref[pl.ds(0, HEADS)].reshape(D, TOK)
        context = jnp.transpose(context_t.astype(F32)).astype(BF)
        valid = valid_ref[...].astype(F32)

        def block(part, half, start, size):
            ref = odd_ref if part % 2 else even_ref
            return ref[half * 8 + part // 2, pl.ds(start, size), :]

        def into(rows, part):
            sides = []
            for unit in range(2):
                low = block(part, 0, unit * D // 2, D // 2)
                high = block(part, 1, unit * D // 2, D // 2)
                sides.append(jnp.concatenate([low, high], axis=0))
            return jnp.dot(rows, jnp.concatenate(sides, axis=1), preferred_element_type=F32)

        attended = jnp.concatenate([into(context, part) for part in range(6, 9)], axis=1)
        hidden = (tokens_ref[...].astype(F32) + valid * attended).astype(BF)
        residual = hidden.astype(F32)
        normed = norm_rows(residual, gain_ref[...].reshape(1, D)).astype(BF)
        inner = jnp.concatenate([jax.nn.gelu(into(normed, part)).astype(BF) for part in range(9, 15)], axis=1)
        for chunk in range(3):
            parts = (2 * chunk, 2 * chunk + 1)
            low = jnp.concatenate([block(part, 0, 0, D) for part in parts], axis=1)
            high = jnp.concatenate([block(part, 1, 0, D) for part in parts], axis=1)
            down = jnp.dot(inner, jnp.concatenate([low, high], axis=0), preferred_element_type=F32)
            span = slice(chunk * WIDE, (chunk + 1) * WIDE)
            out_ref[:, span] = (residual[:, span] + valid * down).astype(BF)

    @pl.when(core == 0)
    def _():
        run(near_ref, far_ref)

    @pl.when(core == 1)
    def _():
        run(far_ref, near_ref)


def body(tokens, patch_valid, block_mask, gain_attn, gain_mlp, w_qkv, w_out, w_up, w_down):
    lat_rows, lon_cols = tokens.shape[0], tokens.shape[1]
    own = tokens.reshape(TOK, D)
    normed, piece = pl.pallas_call(
        prepare,
        out_shape=(
            jax.ShapeDtypeStruct((TOK + 8, D), BF),
            jax.ShapeDtypeStruct((96, LANES), BF),
        ),
        in_specs=[whole()] * 7,
        out_specs=(whole(),) * 2,
        compiler_params=params(56),
        name="prepare",
    )(own, gain_attn, block_mask, w_qkv, w_out, w_up, w_down)
    strip = lax.all_gather(normed, LON, axis=0)
    rows = lax.all_gather(piece, "z", axis=0)
    mlp_rows, head_half = pl.pallas_call(
        sort_rows,
        out_shape=(
            jax.ShapeDtypeStruct((16, D, LANES), BF),
            jax.ShapeDtypeStruct((D // 2, 2 * LANES), BF),
        ),
        in_specs=[whole()],
        out_specs=(pl.BlockSpec(memory_space=pl.ANY), whole()),
        scratch_shapes=[pltpu.VMEM((D, LANES), BF), pltpu.SemaphoreType.DMA((16,))],
        compiler_params=params(56),
        name="sort_rows",
    )(rows)
    near = lax.all_to_all(mlp_rows, PLANE, 0, 0)
    twin = lax.ppermute(head_half, "xh", [(0, 1), (1, 0)])
    halo = jax.ShapeDtypeStruct((LANES, 4 * LANES), BF)
    keys = STRIPES * TOK
    q_t, k_n, v_t, to_up, to_down, bias = pl.pallas_call(
        project,
        out_shape=(
            jax.ShapeDtypeStruct((HEAD, keys), BF),
            jax.ShapeDtypeStruct((keys, HEAD), BF),
            jax.ShapeDtypeStruct((HEAD, keys), BF),
            halo,
            halo,
            jax.ShapeDtypeStruct((STRIPES, keys), F32),
        ),
        in_specs=[whole()] * 3,
        out_specs=(whole(),) * 6,
        compiler_params=params(14),
        cost_estimate=pl.CostEstimate(flops=2 * 2048 * 768 * 256, bytes_accessed=5 << 20, transcendentals=0),
        name="project",
    )(strip, head_half, twin)
    above = lax.ppermute(to_down, LAT, [(i, i + 1) for i in range(31)])
    below = lax.ppermute(to_up, LAT, [(i + 1, i) for i in range(31)])

    stat = jax.ShapeDtypeStruct((8, keys), F32)
    acc, peaks, sums = pl.pallas_call(
        attend_strip,
        out_shape=(jax.ShapeDtypeStruct((HEAD, keys), F32), stat, stat),
        in_specs=[whole()] * 4,
        out_specs=(whole(),) * 3,
        scratch_shapes=[
            pltpu.VMEM((8, WIDE, WIDE), F32),
            pltpu.VMEM((8, WIDE, WIDE), F32),
            pltpu.VMEM((8, WIDE), F32),
            pltpu.VMEM((8, WIDE), F32),
        ],
        compiler_params=params(14),
        cost_estimate=pl.CostEstimate(
            flops=4 * 2048 * 2048 * 256, bytes_accessed=3 << 20, transcendentals=2048 * 2048
        ),
        name="attend_strip",
    )(q_t, k_n, v_t, bias)

    context = pl.pallas_call(
        attend_edges,
        out_shape=jax.ShapeDtypeStruct((STRIPES, HEAD, TOK), BF),
        in_specs=[whole()] * 6,
        out_specs=whole(),
        compiler_params=params(8),
        name="attend_edges",
    )(q_t, above, below, acc, peaks, sums)

    near, context = lax.optimization_barrier((near, context))
    far = lax.ppermute(near, "c", [(0, 1), (1, 0)])
    mine = lax.all_to_all(context, LON, 0, 0)
    mixed = pl.pallas_call(
        finish,
        out_shape=jax.ShapeDtypeStruct((TOK, D), BF),
        in_specs=[whole()] * 6,
        out_specs=whole(),
        compiler_params=params(20),
        cost_estimate=pl.CostEstimate(flops=2 * 128 * 768 * 3840, bytes_accessed=7 << 20, transcendentals=128 * 1536),
        name="finish",
    )(mine, near, far, own, patch_valid.reshape(TOK, 1), gain_mlp)
    return mixed.reshape(lat_rows, lon_cols, D)


def solution(mesh):
    fine = Mesh(mesh.devices.reshape(4, 2, 2, 2, 16), ("y", "xl", "c", "xh", "z"))
    in_specs = (
        P(LAT, LON, None),
        P(LAT, LON),
        P(LAT, LON, None),
        P(),
        P(),
        P(LAT, None),
        P(LAT, None),
        P(LAT, None),
        P(LAT, None),
    )
    out_specs = P(LAT, LON, None)
    return jax.shard_map(body, mesh=fine, in_specs=in_specs, out_specs=out_specs, check_vma=False)
```

```python
import functools

import jax
import jax.numpy as jnp
from jax import lax
from jax.experimental import pallas as pl
from jax.experimental.pallas import tpu as pltpu
from jax.sharding import Mesh, PartitionSpec as P

D = 768
HEADS = 12
HEAD = 64
FFW = 1536
TOK = 128
STRIPES = 16
LANES = 128
EDGE = 32
WIDE = 256
SPLIT = 480
MASKED = -1e30
LON = ("y", "xl", "c")
CHIPS = ("y", "xl")
LAT = ("xh", "z")
BF = jnp.bfloat16
F32 = jnp.float32


def norm_rows(x, gain):
    centre = jnp.mean(x, axis=-1, keepdims=True)
    diff = x - centre
    spread = jnp.mean(diff * diff, axis=-1, keepdims=True)
    return diff * lax.rsqrt(spread + 1e-05) * gain


def params(mib):
    return pltpu.CompilerParams(vmem_limit_bytes=mib << 20)


def whole():
    return pl.BlockSpec(memory_space=pltpu.VMEM)


def lon_place():
    return (lax.axis_index("y") * 2 + lax.axis_index("xl")) * 2 + lax.axis_index("c")


def prepare(tokens_ref, gain_ref, mask_ref, qkv_ref, out_ref, up_ref, down_ref, norm_out, piece_out):
    norm_out[pl.ds(0, TOK), :] = norm_rows(
        tokens_ref[...].astype(F32), gain_ref[...].reshape(1, D)
    ).astype(BF)
    seen = jnp.broadcast_to(mask_ref[0].astype(F32), (8, STRIPES))
    norm_out[pl.ds(TOK, 8), :] = jnp.concatenate([seen, jnp.zeros((8, D - STRIPES), F32)], axis=1).astype(BF)

    place_j = lon_place()
    head = lax.rem(place_j, HEADS)
    block = head // 2
    odd = lax.rem(head, 2) == 1
    parts = []
    for which in range(3):
        start = pl.multiple_of(which * D + block * LANES, LANES)
        pair = qkv_ref[:, pl.ds(start, LANES)].astype(F32)
        parts.append(jnp.where(odd, pltpu.roll(pair, HEAD, 1), pair))
    low = lax.broadcasted_iota(jnp.int32, (24, LANES), 1) < HEAD
    qk = jnp.where(low, parts[0], pltpu.roll(parts[1], HEAD, 1)).astype(BF)
    v = jnp.where(low, parts[2], 0.0).astype(BF)
    piece_out[pl.ds(0, 24), :] = qk
    piece_out[pl.ds(24, 24), :] = v

    def fill(top, bottom):
        piece_out[pl.ds(48, 24), :] = top
        piece_out[pl.ds(72, 24), :] = bottom

    @pl.when(place_j < 6)
    def _():
        span = pl.ds(pl.multiple_of(place_j * LANES, LANES), LANES)
        fill(down_ref[pl.ds(0, 24), span], down_ref[pl.ds(24, 24), span])

    @pl.when((place_j >= 6) & (place_j < 9))
    def _():
        start = pl.multiple_of((place_j - 6) * 2 * LANES, LANES)
        fill(out_ref[:, pl.ds(start, LANES)], out_ref[:, pl.ds(start + LANES, LANES)])

    @pl.when(place_j >= 9)
    def _():
        start = pl.multiple_of(jnp.minimum(place_j - 9, 5) * 2 * LANES, LANES)
        fill(up_ref[:, pl.ds(start, LANES)], up_ref[:, pl.ds(start + LANES, LANES)])


def sort_gather(rows_ref, order_ref, gather_out):
    place_j = lon_place()
    xh = lax.axis_index("xh")

    @pl.when(place_j < 6)
    def _():
        for part in range(SPLIT // 48):
            gather_out[pl.ds(part * 48, 48), :] = rows_ref[part % 16, xh, pl.ds(48, 48), :]

    @pl.when(place_j >= 6)
    def _():
        for part in range(SPLIT // 24):
            source = rows_ref.at[part % 16, (part // 16) ^ xh]
            gather_out[pl.ds(part * 24, 24), :] = source[pl.ds(48, 24), :]


def sort_spread(rows_ref, spread_hbm, rest, sems):
    place_j = lon_place()
    xh = lax.axis_index("xh")

    @pl.when(place_j < 6)
    def _():
        for part in range(SPLIT // 48, 32):
            source = rows_ref.at[part % 16, (part // 16) ^ xh]
            rest[pl.ds(part * 48 - SPLIT, 48), :] = source[pl.ds(48, 48), :]

    @pl.when(place_j >= 6)
    def _():
        for part in range(32):
            source = rows_ref.at[part % 16, (part // 16) ^ xh]
            if part * 24 >= SPLIT:
                rest[pl.ds(part * 24 - SPLIT, 24), :] = source[pl.ds(48, 24), :]
            rest[pl.ds(D - SPLIT + part * 24, 24), :] = source[pl.ds(72, 24), :]

    copies = [pltpu.make_async_copy(rest, spread_hbm.at[peer], sems.at[peer]) for peer in range(8)]
    for copy in copies:
        copy.start()
    for copy in copies:
        copy.wait()


def sort_head(rows_ref, head_out):
    xh = lax.axis_index("xh")
    for part in range(32):
        source = rows_ref.at[part % 16, (part // 16) ^ xh]
        head_out[pl.ds(part * 24, 24), pl.ds(0, LANES)] = source[pl.ds(0, 24), :]
        head_out[pl.ds(part * 24, 24), pl.ds(LANES, LANES)] = source[pl.ds(24, 24), :]


def project(strip_ref, weight_ref, q_out, k_out, vt_out, up_out, down_out, bias_out):
    weight = weight_ref[...]
    tops = []
    ends = []
    for tile in range(STRIPES):
        full = jnp.dot(strip_ref[tile, pl.ds(0, TOK), :], weight, preferred_element_type=F32)
        qk = full[:, :LANES]
        qk_t = jnp.transpose(qk)
        v_t = jnp.transpose(full[:, LANES:])[:HEAD]
        span = pl.ds(tile * TOK, TOK)
        q_out[:, span] = (qk_t[:HEAD] * HEAD ** (-0.5)).astype(BF)
        k_out[span, :] = qk[:, HEAD:].astype(BF)
        vt_out[:, span] = v_t.astype(BF)
        kv_t = jnp.concatenate([qk_t[HEAD:], v_t], axis=0)
        seen = jnp.broadcast_to(strip_ref[tile, pl.ds(TOK, 8), :LANES].astype(F32)[:1], (LANES, LANES))
        bias_out[:, span] = jnp.where(jnp.transpose(seen)[:STRIPES] > 0, 0.0, MASKED)
        tops.append(kv_t[:, :EDGE])
        ends.append(kv_t[:, TOK - EDGE :])
    for group in range(4):
        span = pl.ds(group * LANES, LANES)
        up_out[:, span] = jnp.concatenate(tops[group * 4 : group * 4 + 4], axis=1).astype(BF)
        down_out[:, span] = jnp.concatenate(ends[group * 4 : group * 4 + 4], axis=1).astype(BF)


def attend_strip(
    q_ref, k_ref, vt_ref, bias_ref, acc_out, max_out, sum_out, even_scores, odd_scores, even_top, odd_top
):
    def score_chunk(group, chunk, scores, top):
        span = pl.ds(pl.multiple_of(group * WIDE, WIDE), WIDE)
        part = jnp.dot(k_ref[pl.ds(chunk * WIDE, WIDE), :], q_ref[:, span], preferred_element_type=F32)
        for half in range(2):
            row = bias_ref[pl.ds(chunk * 2 + half, 1), span]
            piece = part[half * TOK : (half + 1) * TOK] + row
            scores[chunk, pl.ds(half * TOK, TOK), :] = piece
            best = jnp.max(piece.reshape(16, 8, WIDE), axis=0)
            top = best if top is None else jnp.maximum(top, best)
        return top

    def step(group, scores, top_ref, coming, next_scores, next_top):
        peak = jnp.max(top_ref[...], axis=0, keepdims=True)
        total = jnp.zeros((8, WIDE), F32)
        acc = jnp.zeros((HEAD, WIDE), F32)
        top = None
        for chunk in range(8):
            top = score_chunk(coming, chunk, next_scores, top)
            weights = jnp.exp(scores[chunk] - peak)
            total = total + jnp.sum(weights.reshape(32, 8, WIDE), axis=0)
            acc = acc + jnp.dot(
                vt_ref[:, pl.ds(chunk * WIDE, WIDE)], weights.astype(BF), preferred_element_type=F32
            )
        next_top[...] = top
        span = pl.ds(pl.multiple_of(group * WIDE, WIDE), WIDE)
        acc_out[:, span] = acc
        max_out[:, span] = jnp.broadcast_to(peak, (8, WIDE))
        sum_out[:, span] = jnp.broadcast_to(jnp.sum(total, axis=0, keepdims=True), (8, WIDE))

    top = None
    for chunk in range(8):
        top = score_chunk(0, chunk, even_scores, top)
    even_top[...] = top

    def pair(index, carry):
        first = index * 2
        step(first, even_scores, even_top, first + 1, odd_scores, odd_top)
        step(first + 1, odd_scores, odd_top, jnp.minimum(first + 2, 7), even_scores, even_top)
        return carry

    lax.fori_loop(0, 4, pair, 0)


def attend_edges(q_ref, above_ref, below_ref, acc_ref, max_ref, sum_ref, out_ref):
    row = lax.axis_index("xh") * 16 + lax.axis_index("z")
    key_band = lax.broadcasted_iota(jnp.int32, (LANES, 4 * TOK), 0) // EDGE
    query_band = lax.broadcasted_iota(jnp.int32, (LANES, 4 * TOK), 1) // TOK
    same = key_band == query_band
    for group in range(4):
        wide = slice(group * 4 * TOK, (group + 1) * 4 * TOK)
        keys = slice(group * LANES, (group + 1) * LANES)
        queries = q_ref[:, wide]
        scores = []
        for ref, flag in ((above_ref, row > 0), (below_ref, row < 31)):
            part = lax.dot_general(
                ref[:HEAD, keys], queries, (((0,), (0,)), ((), ())), preferred_element_type=F32
            )
            scores.append(jnp.where(same & flag, part, MASKED))
        old = max_ref[:1, wide]
        peak = jnp.maximum(old, jnp.max(jnp.maximum(scores[0], scores[1]), axis=0, keepdims=True))
        factor = jnp.exp(old - peak)
        acc = acc_ref[:, wide] * factor
        total = sum_ref[:1, wide] * factor
        for ref, part in ((above_ref, scores[0]), (below_ref, scores[1])):
            weights = jnp.exp(part - peak)
            total = total + jnp.sum(weights, axis=0, keepdims=True)
            acc = acc + jnp.dot(ref[HEAD:, keys], weights.astype(BF), preferred_element_type=F32)
        result = (acc / total).astype(BF)
        for index in range(4):
            out_ref[group * 4 + index] = result[:, index * TOK : (index + 1) * TOK]


def finish(ctx_ref, gather_ref, near_ref, far_ref, tokens_ref, valid_ref, gain_ref, out_ref):
    core = lax.axis_index("c")

    def run(even_ref, odd_ref):
        context_t = ctx_ref[pl.ds(0, HEADS)].reshape(D, TOK)
        context = jnp.transpose(context_t.astype(F32)).astype(BF)
        valid = valid_ref[...].astype(F32)

        def column(part):
            ref = odd_ref if part % 2 else even_ref
            return [gather_ref[part], ref[part // 2]]

        def into(rows, part):
            head, rest = column(part)
            left = jnp.concatenate([head, rest[: D - SPLIT]], axis=0)
            weight = jnp.concatenate([left, rest[D - SPLIT :]], axis=1)
            return jnp.dot(rows, weight, preferred_element_type=F32)

        attended = jnp.concatenate([into(context, part) for part in range(6, 9)], axis=1)
        hidden = (tokens_ref[...].astype(F32) + valid * attended).astype(BF)
        residual = hidden.astype(F32)
        normed = norm_rows(residual, gain_ref[...].reshape(1, D)).astype(BF)
        inner = jnp.concatenate([jax.nn.gelu(into(normed, part)).astype(BF) for part in range(9, 15)], axis=1)
        for chunk in range(3):
            weight = jnp.concatenate(
                [jnp.concatenate(column(2 * chunk + side), axis=0) for side in range(2)], axis=1
            )
            down = jnp.dot(inner, weight, preferred_element_type=F32)
            span = slice(chunk * WIDE, (chunk + 1) * WIDE)
            out_ref[:, span] = (residual[:, span] + valid * down).astype(BF)

    @pl.when(core == 0)
    def _():
        run(near_ref, far_ref)

    @pl.when(core == 1)
    def _():
        run(far_ref, near_ref)


def body(tokens, patch_valid, block_mask, gain_attn, gain_mlp, w_qkv, w_out, w_up, w_down):
    lat_rows, lon_cols = tokens.shape[0], tokens.shape[1]
    own = tokens.reshape(TOK, D)
    normed, piece = pl.pallas_call(
        prepare,
        out_shape=(
            jax.ShapeDtypeStruct((TOK + 8, D), BF),
            jax.ShapeDtypeStruct((96, LANES), BF),
        ),
        in_specs=[whole()] * 7,
        out_specs=(whole(),) * 2,
        compiler_params=params(56),
        name="prepare",
    )(own, gain_attn, block_mask, w_qkv, w_out, w_up, w_down)
    twin = lax.ppermute(piece, "xh", [(0, 1), (1, 0)])
    strip = lax.all_gather(normed, LON, axis=0)
    both = jnp.stack([piece, twin])
    rows = lax.all_gather(both, "z", axis=0)
    spread_rows = pl.pallas_call(
        sort_spread,
        out_shape=jax.ShapeDtypeStruct((8, FFW - SPLIT, LANES), BF),
        in_specs=[whole()],
        out_specs=pl.BlockSpec(memory_space=pl.ANY),
        scratch_shapes=[pltpu.VMEM((FFW - SPLIT, LANES), BF), pltpu.SemaphoreType.DMA((8,))],
        compiler_params=params(56),
        name="sort_spread",
    )(rows)
    near = lax.all_to_all(spread_rows, CHIPS, 0, 0)
    gather_rows = pl.pallas_call(
        sort_gather,
        out_shape=jax.ShapeDtypeStruct((SPLIT, LANES), BF),
        in_specs=[whole(), pl.BlockSpec(memory_space=pl.ANY)],
        out_specs=whole(),
        compiler_params=params(56),
        name="sort_gather",
    )(rows, spread_rows)
    gathered = lax.all_gather(gather_rows, LON, axis=0)
    head_w = pl.pallas_call(
        sort_head,
        out_shape=jax.ShapeDtypeStruct((D, 2 * LANES), BF),
        in_specs=[whole()],
        out_specs=whole(),
        compiler_params=params(56),
        name="sort_head",
    )(rows)
    halo = jax.ShapeDtypeStruct((LANES, 4 * LANES), BF)
    keys = STRIPES * TOK
    q_t, k_n, v_t, to_up, to_down, bias = pl.pallas_call(
        project,
        out_shape=(
            jax.ShapeDtypeStruct((HEAD, keys), BF),
            jax.ShapeDtypeStruct((keys, HEAD), BF),
            jax.ShapeDtypeStruct((HEAD, keys), BF),
            halo,
            halo,
            jax.ShapeDtypeStruct((STRIPES, keys), F32),
        ),
        in_specs=[whole()] * 2,
        out_specs=(whole(),) * 6,
        compiler_params=params(14),
        cost_estimate=pl.CostEstimate(flops=2 * 2048 * 768 * 256, bytes_accessed=5 << 20, transcendentals=0),
        name="project",
    )(strip, head_w)
    above = lax.ppermute(to_down, LAT, [(i, i + 1) for i in range(31)])
    below = lax.ppermute(to_up, LAT, [(i + 1, i) for i in range(31)])

    stat = jax.ShapeDtypeStruct((8, keys), F32)
    acc, peaks, sums = pl.pallas_call(
        attend_strip,
        out_shape=(jax.ShapeDtypeStruct((HEAD, keys), F32), stat, stat),
        in_specs=[whole()] * 4,
        out_specs=(whole(),) * 3,
        scratch_shapes=[
            pltpu.VMEM((8, WIDE, WIDE), F32),
            pltpu.VMEM((8, WIDE, WIDE), F32),
            pltpu.VMEM((8, WIDE), F32),
            pltpu.VMEM((8, WIDE), F32),
        ],
        compiler_params=params(14),
        cost_estimate=pl.CostEstimate(
            flops=4 * 2048 * 2048 * 256, bytes_accessed=3 << 20, transcendentals=2048 * 2048
        ),
        name="attend_strip",
    )(q_t, k_n, v_t, bias)

    context = pl.pallas_call(
        attend_edges,
        out_shape=jax.ShapeDtypeStruct((STRIPES, HEAD, TOK), BF),
        in_specs=[whole()] * 6,
        out_specs=whole(),
        compiler_params=params(8),
        name="attend_edges",
    )(q_t, above, below, acc, peaks, sums)

    near, context = lax.optimization_barrier((near, context))
    far = lax.ppermute(near, "c", [(0, 1), (1, 0)])
    mine = lax.all_to_all(context, LON, 0, 0)
    mixed = pl.pallas_call(
        finish,
        out_shape=jax.ShapeDtypeStruct((TOK, D), BF),
        in_specs=[whole()] * 7,
        out_specs=whole(),
        compiler_params=params(20),
        cost_estimate=pl.CostEstimate(flops=2 * 128 * 768 * 3840, bytes_accessed=7 << 20, transcendentals=128 * 1536),
        name="finish",
    )(mine, gathered, near, far, own, patch_valid.reshape(TOK, 1), gain_mlp)
    return mixed.reshape(lat_rows, lon_cols, D)


def solution(mesh):
    fine = Mesh(mesh.devices.reshape(4, 2, 2, 2, 16), ("y", "xl", "c", "xh", "z"))
    in_specs = (
        P(LAT, LON, None),
        P(LAT, LON),
        P(LAT, LON, None),
        P(),
        P(),
        P(LAT, None),
        P(LAT, None),
        P(LAT, None),
        P(LAT, None),
    )
    out_specs = P(LAT, LON, None)
    return jax.shard_map(body, mesh=fine, in_specs=in_specs, out_specs=out_specs, check_vma=False)
```

```python
import functools

import jax
import jax.numpy as jnp
from jax import lax
from jax.experimental import pallas as pl
from jax.experimental.pallas import tpu as pltpu
from jax.sharding import Mesh, PartitionSpec as P

D = 768
HEADS = 12
HEAD = 64
FFW = 1536
TOK = 128
STRIPES = 16
LANES = 128
EDGE = 32
WIDE = 256
SPLIT = 528
MASKED = -1e30
LON = ("y", "xl", "c")
CHIPS = ("y", "xl")
LAT = ("xh", "z")
BF = jnp.bfloat16
F32 = jnp.float32


def norm_rows(x, gain):
    centre = jnp.mean(x, axis=-1, keepdims=True)
    diff = x - centre
    spread = jnp.mean(diff * diff, axis=-1, keepdims=True)
    return diff * lax.rsqrt(spread + 1e-05) * gain


def params(mib):
    return pltpu.CompilerParams(vmem_limit_bytes=mib << 20)


def whole():
    return pl.BlockSpec(memory_space=pltpu.VMEM)


def lon_place():
    return (lax.axis_index("y") * 2 + lax.axis_index("xl")) * 2 + lax.axis_index("c")


def prepare(tokens_ref, gain_ref, mask_ref, qkv_ref, out_ref, up_ref, down_ref, norm_out, piece_out):
    norm_out[pl.ds(0, TOK), :] = norm_rows(
        tokens_ref[...].astype(F32), gain_ref[...].reshape(1, D)
    ).astype(BF)
    seen = jnp.broadcast_to(mask_ref[0].astype(F32), (8, STRIPES))
    norm_out[pl.ds(TOK, 8), :] = jnp.concatenate([seen, jnp.zeros((8, D - STRIPES), F32)], axis=1).astype(BF)

    place_j = lon_place()
    head = lax.rem(place_j, HEADS)
    block = head // 2
    odd = lax.rem(head, 2) == 1
    parts = []
    for which in range(3):
        start = pl.multiple_of(which * D + block * LANES, LANES)
        pair = qkv_ref[:, pl.ds(start, LANES)].astype(F32)
        parts.append(jnp.where(odd, pltpu.roll(pair, HEAD, 1), pair))
    low = lax.broadcasted_iota(jnp.int32, (24, LANES), 1) < HEAD
    qk = jnp.where(low, parts[0], pltpu.roll(parts[1], HEAD, 1)).astype(BF)
    v = jnp.where(low, parts[2], 0.0).astype(BF)
    piece_out[pl.ds(0, 24), :] = qk
    piece_out[pl.ds(24, 24), :] = v

    def fill(top, bottom):
        piece_out[pl.ds(48, 24), :] = top
        piece_out[pl.ds(72, 24), :] = bottom

    @pl.when(place_j < 6)
    def _():
        span = pl.ds(pl.multiple_of(place_j * LANES, LANES), LANES)
        fill(down_ref[pl.ds(0, 24), span], down_ref[pl.ds(24, 24), span])

    @pl.when((place_j >= 6) & (place_j < 9))
    def _():
        start = pl.multiple_of((place_j - 6) * 2 * LANES, LANES)
        fill(out_ref[:, pl.ds(start, LANES)], out_ref[:, pl.ds(start + LANES, LANES)])

    @pl.when(place_j >= 9)
    def _():
        start = pl.multiple_of(jnp.minimum(place_j - 9, 5) * 2 * LANES, LANES)
        fill(up_ref[:, pl.ds(start, LANES)], up_ref[:, pl.ds(start + LANES, LANES)])


def sort_gather(rows_ref, gather_out):
    place_j = lon_place()
    xh = lax.axis_index("xh")

    @pl.when(place_j < 6)
    def _():
        for part in range(SPLIT // 48):
            gather_out[pl.ds(part * 48, 48), :] = rows_ref[part % 16, xh, pl.ds(48, 48), :]

    @pl.when(place_j >= 6)
    def _():
        for part in range(SPLIT // 24):
            source = rows_ref.at[part % 16, (part // 16) ^ xh]
            gather_out[pl.ds(part * 24, 24), :] = source[pl.ds(48, 24), :]


def sort_spread(rows_ref, order_ref, spread_hbm, rest, sems):
    place_j = lon_place()
    xh = lax.axis_index("xh")

    @pl.when(place_j < 6)
    def _():
        for part in range(SPLIT // 48, 32):
            source = rows_ref.at[part % 16, (part // 16) ^ xh]
            rest[pl.ds(part * 48 - SPLIT, 48), :] = source[pl.ds(48, 48), :]

    @pl.when(place_j >= 6)
    def _():
        for part in range(32):
            source = rows_ref.at[part % 16, (part // 16) ^ xh]
            if part * 24 >= SPLIT:
                rest[pl.ds(part * 24 - SPLIT, 24), :] = source[pl.ds(48, 24), :]
            rest[pl.ds(D - SPLIT + part * 24, 24), :] = source[pl.ds(72, 24), :]

    copies = [pltpu.make_async_copy(rest, spread_hbm.at[peer], sems.at[peer]) for peer in range(8)]
    for copy in copies:
        copy.start()
    for copy in copies:
        copy.wait()


def sort_head(rows_ref, head_out):
    xh = lax.axis_index("xh")
    for part in range(32):
        source = rows_ref.at[part % 16, (part // 16) ^ xh]
        head_out[pl.ds(part * 24, 24), pl.ds(0, LANES)] = source[pl.ds(0, 24), :]
        head_out[pl.ds(part * 24, 24), pl.ds(LANES, LANES)] = source[pl.ds(24, 24), :]


def project(strip_ref, weight_ref, q_out, k_out, vt_out, up_out, down_out, bias_out):
    weight = weight_ref[...]
    tops = []
    ends = []
    for tile in range(STRIPES):
        full = jnp.dot(strip_ref[tile, pl.ds(0, TOK), :], weight, preferred_element_type=F32)
        qk = full[:, :LANES]
        qk_t = jnp.transpose(qk)
        v_t = jnp.transpose(full[:, LANES:])[:HEAD]
        span = pl.ds(tile * TOK, TOK)
        q_out[:, span] = (qk_t[:HEAD] * HEAD ** (-0.5)).astype(BF)
        k_out[span, :] = qk[:, HEAD:].astype(BF)
        vt_out[:, span] = v_t.astype(BF)
        kv_t = jnp.concatenate([qk_t[HEAD:], v_t], axis=0)
        seen = jnp.broadcast_to(strip_ref[tile, pl.ds(TOK, 8), :LANES].astype(F32)[:1], (LANES, LANES))
        bias_out[:, span] = jnp.where(jnp.transpose(seen)[:STRIPES] > 0, 0.0, MASKED)
        tops.append(kv_t[:, :EDGE])
        ends.append(kv_t[:, TOK - EDGE :])
    for group in range(4):
        span = pl.ds(group * LANES, LANES)
        up_out[:, span] = jnp.concatenate(tops[group * 4 : group * 4 + 4], axis=1).astype(BF)
        down_out[:, span] = jnp.concatenate(ends[group * 4 : group * 4 + 4], axis=1).astype(BF)


def attend_strip(
    q_ref, k_ref, vt_ref, bias_ref, acc_out, max_out, sum_out, even_scores, odd_scores, even_top, odd_top
):
    def score_chunk(group, chunk, scores, top):
        span = pl.ds(pl.multiple_of(group * WIDE, WIDE), WIDE)
        part = jnp.dot(k_ref[pl.ds(chunk * WIDE, WIDE), :], q_ref[:, span], preferred_element_type=F32)
        for half in range(2):
            row = bias_ref[pl.ds(chunk * 2 + half, 1), span]
            piece = part[half * TOK : (half + 1) * TOK] + row
            scores[chunk, pl.ds(half * TOK, TOK), :] = piece
            best = jnp.max(piece.reshape(16, 8, WIDE), axis=0)
            top = best if top is None else jnp.maximum(top, best)
        return top

    def step(group, scores, top_ref, coming, next_scores, next_top):
        peak = jnp.max(top_ref[...], axis=0, keepdims=True)
        total = jnp.zeros((8, WIDE), F32)
        acc = jnp.zeros((HEAD, WIDE), F32)
        top = None
        for chunk in range(8):
            top = score_chunk(coming, chunk, next_scores, top)
            weights = jnp.exp(scores[chunk] - peak)
            total = total + jnp.sum(weights.reshape(32, 8, WIDE), axis=0)
            acc = acc + jnp.dot(
                vt_ref[:, pl.ds(chunk * WIDE, WIDE)], weights.astype(BF), preferred_element_type=F32
            )
        next_top[...] = top
        span = pl.ds(pl.multiple_of(group * WIDE, WIDE), WIDE)
        acc_out[:, span] = acc
        max_out[:, span] = jnp.broadcast_to(peak, (8, WIDE))
        sum_out[:, span] = jnp.broadcast_to(jnp.sum(total, axis=0, keepdims=True), (8, WIDE))

    top = None
    for chunk in range(8):
        top = score_chunk(0, chunk, even_scores, top)
    even_top[...] = top

    def pair(index, carry):
        first = index * 2
        step(first, even_scores, even_top, first + 1, odd_scores, odd_top)
        step(first + 1, odd_scores, odd_top, jnp.minimum(first + 2, 7), even_scores, even_top)
        return carry

    lax.fori_loop(0, 4, pair, 0)


def attend_edges(q_ref, above_ref, below_ref, acc_ref, max_ref, sum_ref, out_ref):
    row = lax.axis_index("xh") * 16 + lax.axis_index("z")
    key_band = lax.broadcasted_iota(jnp.int32, (LANES, 4 * TOK), 0) // EDGE
    query_band = lax.broadcasted_iota(jnp.int32, (LANES, 4 * TOK), 1) // TOK
    same = key_band == query_band
    for group in range(4):
        wide = slice(group * 4 * TOK, (group + 1) * 4 * TOK)
        keys = slice(group * LANES, (group + 1) * LANES)
        queries = q_ref[:, wide]
        scores = []
        for ref, flag in ((above_ref, row > 0), (below_ref, row < 31)):
            part = lax.dot_general(
                ref[:HEAD, keys], queries, (((0,), (0,)), ((), ())), preferred_element_type=F32
            )
            scores.append(jnp.where(same & flag, part, MASKED))
        old = max_ref[:1, wide]
        peak = jnp.maximum(old, jnp.max(jnp.maximum(scores[0], scores[1]), axis=0, keepdims=True))
        factor = jnp.exp(old - peak)
        acc = acc_ref[:, wide] * factor
        total = sum_ref[:1, wide] * factor
        for ref, part in ((above_ref, scores[0]), (below_ref, scores[1])):
            weights = jnp.exp(part - peak)
            total = total + jnp.sum(weights, axis=0, keepdims=True)
            acc = acc + jnp.dot(ref[HEAD:, keys], weights.astype(BF), preferred_element_type=F32)
        result = (acc / total).astype(BF)
        for index in range(4):
            out_ref[group * 4 + index] = result[:, index * TOK : (index + 1) * TOK]


def finish(ctx_ref, gather_ref, near_ref, far_ref, tokens_ref, valid_ref, gain_ref, out_ref):
    core = lax.axis_index("c")

    def run(even_ref, odd_ref):
        context_t = ctx_ref[pl.ds(0, HEADS)].reshape(D, TOK)
        context = jnp.transpose(context_t.astype(F32)).astype(BF)
        valid = valid_ref[...].astype(F32)

        def column(part):
            ref = odd_ref if part % 2 else even_ref
            return [gather_ref[part], ref[part // 2]]

        def into(rows, part):
            head, rest = column(part)
            left = jnp.concatenate([head, rest[: D - SPLIT]], axis=0)
            weight = jnp.concatenate([left, rest[D - SPLIT :]], axis=1)
            return jnp.dot(rows, weight, preferred_element_type=F32)

        attended = jnp.concatenate([into(context, part) for part in range(6, 9)], axis=1)
        hidden = (tokens_ref[...].astype(F32) + valid * attended).astype(BF)
        residual = hidden.astype(F32)
        normed = norm_rows(residual, gain_ref[...].reshape(1, D)).astype(BF)
        inner = jnp.concatenate([jax.nn.gelu(into(normed, part)).astype(BF) for part in range(9, 15)], axis=1)
        for chunk in range(3):
            weight = jnp.concatenate(
                [jnp.concatenate(column(2 * chunk + side), axis=0) for side in range(2)], axis=1
            )
            down = jnp.dot(inner, weight, preferred_element_type=F32)
            span = slice(chunk * WIDE, (chunk + 1) * WIDE)
            out_ref[:, span] = (residual[:, span] + valid * down).astype(BF)

    @pl.when(core == 0)
    def _():
        run(near_ref, far_ref)

    @pl.when(core == 1)
    def _():
        run(far_ref, near_ref)


def body(tokens, patch_valid, block_mask, gain_attn, gain_mlp, w_qkv, w_out, w_up, w_down):
    lat_rows, lon_cols = tokens.shape[0], tokens.shape[1]
    own = tokens.reshape(TOK, D)
    normed, piece = pl.pallas_call(
        prepare,
        out_shape=(
            jax.ShapeDtypeStruct((TOK + 8, D), BF),
            jax.ShapeDtypeStruct((96, LANES), BF),
        ),
        in_specs=[whole()] * 7,
        out_specs=(whole(),) * 2,
        compiler_params=params(56),
        name="prepare",
    )(own, gain_attn, block_mask, w_qkv, w_out, w_up, w_down)
    twin = lax.ppermute(piece, "xh", [(0, 1), (1, 0)])
    strip = lax.all_gather(normed, LON, axis=0)
    both = jnp.stack([piece, twin])
    rows = lax.all_gather(both, "z", axis=0)
    gather_rows = pl.pallas_call(
        sort_gather,
        out_shape=jax.ShapeDtypeStruct((SPLIT, LANES), BF),
        in_specs=[whole()],
        out_specs=whole(),
        compiler_params=params(6),
        name="sort_gather",
    )(rows)
    gathered = lax.all_gather(gather_rows, LON, axis=0)
    spread_rows = pl.pallas_call(
        sort_spread,
        out_shape=jax.ShapeDtypeStruct((8, FFW - SPLIT, LANES), BF),
        in_specs=[whole(), pl.BlockSpec(memory_space=pl.ANY)],
        out_specs=pl.BlockSpec(memory_space=pl.ANY),
        scratch_shapes=[pltpu.VMEM((FFW - SPLIT, LANES), BF), pltpu.SemaphoreType.DMA((8,))],
        compiler_params=params(6),
        name="sort_spread",
    )(rows, gather_rows)
    near = lax.all_to_all(spread_rows, CHIPS, 0, 0)
    head_w = pl.pallas_call(
        sort_head,
        out_shape=jax.ShapeDtypeStruct((D, 2 * LANES), BF),
        in_specs=[whole()],
        out_specs=whole(),
        compiler_params=params(6),
        name="sort_head",
    )(rows)
    halo = jax.ShapeDtypeStruct((LANES, 4 * LANES), BF)
    keys = STRIPES * TOK
    q_t, k_n, v_t, to_up, to_down, bias = pl.pallas_call(
        project,
        out_shape=(
            jax.ShapeDtypeStruct((HEAD, keys), BF),
            jax.ShapeDtypeStruct((keys, HEAD), BF),
            jax.ShapeDtypeStruct((HEAD, keys), BF),
            halo,
            halo,
            jax.ShapeDtypeStruct((STRIPES, keys), F32),
        ),
        in_specs=[whole()] * 2,
        out_specs=(whole(),) * 6,
        compiler_params=params(14),
        cost_estimate=pl.CostEstimate(flops=2 * 2048 * 768 * 256, bytes_accessed=5 << 20, transcendentals=0),
        name="project",
    )(strip, head_w)
    above = lax.ppermute(to_down, LAT, [(i, i + 1) for i in range(31)])
    below = lax.ppermute(to_up, LAT, [(i + 1, i) for i in range(31)])

    stat = jax.ShapeDtypeStruct((8, keys), F32)
    acc, peaks, sums = pl.pallas_call(
        attend_strip,
        out_shape=(jax.ShapeDtypeStruct((HEAD, keys), F32), stat, stat),
        in_specs=[whole()] * 4,
        out_specs=(whole(),) * 3,
        scratch_shapes=[
            pltpu.VMEM((8, WIDE, WIDE), F32),
            pltpu.VMEM((8, WIDE, WIDE), F32),
            pltpu.VMEM((8, WIDE), F32),
            pltpu.VMEM((8, WIDE), F32),
        ],
        compiler_params=params(14),
        cost_estimate=pl.CostEstimate(
            flops=4 * 2048 * 2048 * 256, bytes_accessed=3 << 20, transcendentals=2048 * 2048
        ),
        name="attend_strip",
    )(q_t, k_n, v_t, bias)

    context = pl.pallas_call(
        attend_edges,
        out_shape=jax.ShapeDtypeStruct((STRIPES, HEAD, TOK), BF),
        in_specs=[whole()] * 6,
        out_specs=whole(),
        compiler_params=params(8),
        name="attend_edges",
    )(q_t, above, below, acc, peaks, sums)

    near, context = lax.optimization_barrier((near, context))
    far = lax.ppermute(near, "c", [(0, 1), (1, 0)])
    mine = lax.all_to_all(context, LON, 0, 0)
    mixed = pl.pallas_call(
        finish,
        out_shape=jax.ShapeDtypeStruct((TOK, D), BF),
        in_specs=[whole()] * 7,
        out_specs=whole(),
        compiler_params=params(20),
        cost_estimate=pl.CostEstimate(flops=2 * 128 * 768 * 3840, bytes_accessed=7 << 20, transcendentals=128 * 1536),
        name="finish",
    )(mine, gathered, near, far, own, patch_valid.reshape(TOK, 1), gain_mlp)
    return mixed.reshape(lat_rows, lon_cols, D)


def solution(mesh):
    fine = Mesh(mesh.devices.reshape(4, 2, 2, 2, 16), ("y", "xl", "c", "xh", "z"))
    in_specs = (
        P(LAT, LON, None),
        P(LAT, LON),
        P(LAT, LON, None),
        P(),
        P(),
        P(LAT, None),
        P(LAT, None),
        P(LAT, None),
        P(LAT, None),
    )
    out_specs = P(LAT, LON, None)
    return jax.shard_map(body, mesh=fine, in_specs=in_specs, out_specs=out_specs, check_vma=False)
```

```python
import functools

import jax
import jax.numpy as jnp
from jax import lax
from jax.experimental import pallas as pl
from jax.experimental.pallas import tpu as pltpu
from jax.sharding import Mesh, PartitionSpec as P

D = 768
HEADS = 12
HEAD = 64
FFW = 1536
TOK = 128
STRIPES = 16
LANES = 128
EDGE = 32
WIDE = 256
SPLIT = 528
MASKED = -1e30
LON = ("y", "xl", "c")
CHIPS = ("y", "xl")
LAT = ("xh", "z")
BF = jnp.bfloat16
F32 = jnp.float32


def norm_rows(x, gain):
    centre = jnp.mean(x, axis=-1, keepdims=True)
    diff = x - centre
    spread = jnp.mean(diff * diff, axis=-1, keepdims=True)
    return diff * lax.rsqrt(spread + 1e-05) * gain


def params(mib):
    return pltpu.CompilerParams(vmem_limit_bytes=mib << 20)


def whole():
    return pl.BlockSpec(memory_space=pltpu.VMEM)


def lon_place():
    return (lax.axis_index("y") * 2 + lax.axis_index("xl")) * 2 + lax.axis_index("c")


def prepare(tokens_ref, gain_ref, mask_ref, qkv_ref, out_ref, up_ref, down_ref, norm_out, piece_out):
    norm_out[pl.ds(0, TOK), :] = norm_rows(
        tokens_ref[...].astype(F32), gain_ref[...].reshape(1, D)
    ).astype(BF)
    seen = jnp.broadcast_to(mask_ref[0].astype(F32), (8, STRIPES))
    norm_out[pl.ds(TOK, 8), :] = jnp.concatenate([seen, jnp.zeros((8, D - STRIPES), F32)], axis=1).astype(BF)

    place_j = lon_place()
    head = lax.rem(place_j, HEADS)
    block = head // 2
    odd = lax.rem(head, 2) == 1
    parts = []
    for which in range(3):
        start = pl.multiple_of(which * D + block * LANES, LANES)
        pair = qkv_ref[:, pl.ds(start, LANES)].astype(F32)
        parts.append(jnp.where(odd, pltpu.roll(pair, HEAD, 1), pair))
    low = lax.broadcasted_iota(jnp.int32, (24, LANES), 1) < HEAD
    qk = jnp.where(low, parts[0], pltpu.roll(parts[1], HEAD, 1)).astype(BF)
    v = jnp.where(low, parts[2], 0.0).astype(BF)
    piece_out[pl.ds(0, 24), :] = qk
    piece_out[pl.ds(24, 24), :] = v

    def fill(top, bottom):
        piece_out[pl.ds(48, 24), :] = top
        piece_out[pl.ds(72, 24), :] = bottom

    @pl.when(place_j < 6)
    def _():
        span = pl.ds(pl.multiple_of(place_j * LANES, LANES), LANES)
        fill(down_ref[pl.ds(0, 24), span], down_ref[pl.ds(24, 24), span])

    @pl.when((place_j >= 6) & (place_j < 9))
    def _():
        start = pl.multiple_of((place_j - 6) * 2 * LANES, LANES)
        fill(out_ref[:, pl.ds(start, LANES)], out_ref[:, pl.ds(start + LANES, LANES)])

    @pl.when(place_j >= 9)
    def _():
        start = pl.multiple_of(jnp.minimum(place_j - 9, 5) * 2 * LANES, LANES)
        fill(up_ref[:, pl.ds(start, LANES)], up_ref[:, pl.ds(start + LANES, LANES)])


def sort_gather(rows_ref, gather_out):
    place_j = lon_place()
    xh = lax.axis_index("xh")

    @pl.when(place_j < 6)
    def _():
        for part in range(SPLIT // 48):
            gather_out[pl.ds(part * 48, 48), :] = rows_ref[part % 16, xh, pl.ds(48, 48), :]

    @pl.when(place_j >= 6)
    def _():
        for part in range(SPLIT // 24):
            source = rows_ref.at[part % 16, (part // 16) ^ xh]
            gather_out[pl.ds(part * 24, 24), :] = source[pl.ds(48, 24), :]


def sort_spread(rows_ref, order_ref, spread_hbm, rest, sems):
    place_j = lon_place()
    xh = lax.axis_index("xh")

    @pl.when(place_j < 6)
    def _():
        for part in range(SPLIT // 48, 32):
            source = rows_ref.at[part % 16, (part // 16) ^ xh]
            rest[pl.ds(part * 48 - SPLIT, 48), :] = source[pl.ds(48, 48), :]

    @pl.when(place_j >= 6)
    def _():
        for part in range(32):
            source = rows_ref.at[part % 16, (part // 16) ^ xh]
            if part * 24 >= SPLIT:
                rest[pl.ds(part * 24 - SPLIT, 24), :] = source[pl.ds(48, 24), :]
            rest[pl.ds(D - SPLIT + part * 24, 24), :] = source[pl.ds(72, 24), :]

    copies = [pltpu.make_async_copy(rest, spread_hbm.at[peer], sems.at[peer]) for peer in range(8)]
    for copy in copies:
        copy.start()
    for copy in copies:
        copy.wait()


def sort_head(rows_ref, head_out):
    xh = lax.axis_index("xh")
    for part in range(32):
        source = rows_ref.at[part % 16, (part // 16) ^ xh]
        head_out[pl.ds(part * 24, 24), pl.ds(0, LANES)] = source[pl.ds(0, 24), :]
        head_out[pl.ds(part * 24, 24), pl.ds(LANES, LANES)] = source[pl.ds(24, 24), :]


def project(strip_ref, weight_ref, q_out, k_out, vt_out, up_out, down_out, bias_out):
    weight = weight_ref[...]
    tops = []
    ends = []
    for tile in range(STRIPES):
        full = jnp.dot(strip_ref[tile, pl.ds(0, TOK), :], weight, preferred_element_type=F32)
        qk = full[:, :LANES]
        qk_t = jnp.transpose(qk)
        v_t = jnp.transpose(full[:, LANES:])[:HEAD]
        span = pl.ds(tile * TOK, TOK)
        q_out[:, span] = (qk_t[:HEAD] * HEAD ** (-0.5)).astype(BF)
        k_out[span, :] = qk[:, HEAD:].astype(BF)
        vt_out[:, span] = v_t.astype(BF)
        kv_t = jnp.concatenate([qk_t[HEAD:], v_t], axis=0)
        seen = jnp.broadcast_to(strip_ref[tile, pl.ds(TOK, 8), :LANES].astype(F32)[:1], (LANES, LANES))
        bias_out[:, span] = jnp.where(jnp.transpose(seen)[:STRIPES] > 0, 0.0, MASKED)
        tops.append(kv_t[:, :EDGE])
        ends.append(kv_t[:, TOK - EDGE :])
    for group in range(4):
        span = pl.ds(group * LANES, LANES)
        up_out[:, span] = jnp.concatenate(tops[group * 4 : group * 4 + 4], axis=1).astype(BF)
        down_out[:, span] = jnp.concatenate(ends[group * 4 : group * 4 + 4], axis=1).astype(BF)


def attend_strip(
    q_ref, k_ref, vt_ref, bias_ref, acc_out, max_out, sum_out, even_scores, odd_scores, even_top, odd_top
):
    def score_chunk(group, chunk, scores, top):
        span = pl.ds(pl.multiple_of(group * WIDE, WIDE), WIDE)
        part = jnp.dot(k_ref[pl.ds(chunk * WIDE, WIDE), :], q_ref[:, span], preferred_element_type=F32)
        for half in range(2):
            row = bias_ref[pl.ds(chunk * 2 + half, 1), span]
            piece = part[half * TOK : (half + 1) * TOK] + row
            scores[chunk, pl.ds(half * TOK, TOK), :] = piece
            best = jnp.max(piece.reshape(16, 8, WIDE), axis=0)
            top = best if top is None else jnp.maximum(top, best)
        return top

    def step(group, scores, top_ref, coming, next_scores, next_top):
        peak = jnp.max(top_ref[...], axis=0, keepdims=True)
        total = jnp.zeros((8, WIDE), F32)
        acc = jnp.zeros((HEAD, WIDE), F32)
        top = None
        for chunk in range(8):
            top = score_chunk(coming, chunk, next_scores, top)
            weights = jnp.exp(scores[chunk] - peak)
            total = total + jnp.sum(weights.reshape(32, 8, WIDE), axis=0)
            acc = acc + jnp.dot(
                vt_ref[:, pl.ds(chunk * WIDE, WIDE)], weights.astype(BF), preferred_element_type=F32
            )
        next_top[...] = top
        span = pl.ds(pl.multiple_of(group * WIDE, WIDE), WIDE)
        acc_out[:, span] = acc
        max_out[:, span] = jnp.broadcast_to(peak, (8, WIDE))
        sum_out[:, span] = jnp.broadcast_to(jnp.sum(total, axis=0, keepdims=True), (8, WIDE))

    top = None
    for chunk in range(8):
        top = score_chunk(0, chunk, even_scores, top)
    even_top[...] = top

    def pair(index, carry):
        first = index * 2
        step(first, even_scores, even_top, first + 1, odd_scores, odd_top)
        step(first + 1, odd_scores, odd_top, jnp.minimum(first + 2, 7), even_scores, even_top)
        return carry

    lax.fori_loop(0, 4, pair, 0)


def attend_edges(q_ref, above_ref, below_ref, acc_ref, max_ref, sum_ref, out_ref):
    row = lax.axis_index("xh") * 16 + lax.axis_index("z")
    key_band = lax.broadcasted_iota(jnp.int32, (LANES, 4 * TOK), 0) // EDGE
    query_band = lax.broadcasted_iota(jnp.int32, (LANES, 4 * TOK), 1) // TOK
    same = key_band == query_band
    for group in range(4):
        wide = slice(group * 4 * TOK, (group + 1) * 4 * TOK)
        keys = slice(group * LANES, (group + 1) * LANES)
        queries = q_ref[:, wide]
        scores = []
        for ref, flag in ((above_ref, row > 0), (below_ref, row < 31)):
            part = lax.dot_general(
                ref[:HEAD, keys], queries, (((0,), (0,)), ((), ())), preferred_element_type=F32
            )
            scores.append(jnp.where(same & flag, part, MASKED))
        old = max_ref[:1, wide]
        peak = jnp.maximum(old, jnp.max(jnp.maximum(scores[0], scores[1]), axis=0, keepdims=True))
        factor = jnp.exp(old - peak)
        acc = acc_ref[:, wide] * factor
        total = sum_ref[:1, wide] * factor
        for ref, part in ((above_ref, scores[0]), (below_ref, scores[1])):
            weights = jnp.exp(part - peak)
            total = total + jnp.sum(weights, axis=0, keepdims=True)
            acc = acc + jnp.dot(ref[HEAD:, keys], weights.astype(BF), preferred_element_type=F32)
        result = (acc / total).astype(BF)
        for index in range(4):
            out_ref[group * 4 + index] = result[:, index * TOK : (index + 1) * TOK]


def finish(
    ctx_ref, gather_hbm, near_hbm, far_hbm, tokens_ref, valid_ref, gain_ref, out_ref, weights, sems
):
    core = lax.axis_index("c")

    def run(even_hbm, odd_hbm):
        def copies(part):
            rest = odd_hbm if part % 2 else even_hbm
            return (
                pltpu.make_async_copy(
                    gather_hbm.at[part], weights.at[part, pl.ds(0, SPLIT), :], sems.at[2 * part]
                ),
                pltpu.make_async_copy(
                    rest.at[part // 2], weights.at[part, pl.ds(SPLIT, FFW - SPLIT), :], sems.at[2 * part + 1]
                ),
            )

        for part in (6, 7, 8, 9, 10, 11, 12, 13, 14, 0, 1, 2, 3, 4, 5):
            for copy in copies(part):
                copy.start()
        context_t = ctx_ref[pl.ds(0, HEADS)].reshape(D, TOK)
        context = jnp.transpose(context_t.astype(F32)).astype(BF)
        valid = valid_ref[...].astype(F32)

        def settle(part):
            for copy in copies(part):
                copy.wait()

        def into(rows, part):
            settle(part)
            weight = jnp.concatenate([weights[part, :D, :], weights[part, D:, :]], axis=1)
            return jnp.dot(rows, weight, preferred_element_type=F32)

        attended = jnp.concatenate([into(context, part) for part in range(6, 9)], axis=1)
        hidden = (tokens_ref[...].astype(F32) + valid * attended).astype(BF)
        residual = hidden.astype(F32)
        normed = norm_rows(residual, gain_ref[...].reshape(1, D)).astype(BF)
        inner = jnp.concatenate([jax.nn.gelu(into(normed, part)).astype(BF) for part in range(9, 15)], axis=1)
        for chunk in range(3):
            settle(2 * chunk)
            settle(2 * chunk + 1)
            weight = jnp.concatenate([weights[2 * chunk], weights[2 * chunk + 1]], axis=1)
            down = jnp.dot(inner, weight, preferred_element_type=F32)
            span = slice(chunk * WIDE, (chunk + 1) * WIDE)
            out_ref[:, span] = (residual[:, span] + valid * down).astype(BF)

    @pl.when(core == 0)
    def _():
        run(near_hbm, far_hbm)

    @pl.when(core == 1)
    def _():
        run(far_hbm, near_hbm)


def body(tokens, patch_valid, block_mask, gain_attn, gain_mlp, w_qkv, w_out, w_up, w_down):
    lat_rows, lon_cols = tokens.shape[0], tokens.shape[1]
    own = tokens.reshape(TOK, D)
    normed, piece = pl.pallas_call(
        prepare,
        out_shape=(
            jax.ShapeDtypeStruct((TOK + 8, D), BF),
            jax.ShapeDtypeStruct((96, LANES), BF),
        ),
        in_specs=[whole()] * 7,
        out_specs=(whole(),) * 2,
        compiler_params=params(56),
        name="prepare",
    )(own, gain_attn, block_mask, w_qkv, w_out, w_up, w_down)
    twin = lax.ppermute(piece, "xh", [(0, 1), (1, 0)])
    strip = lax.all_gather(normed, LON, axis=0)
    both = jnp.stack([piece, twin])
    rows = lax.all_gather(both, "z", axis=0)
    gather_rows = pl.pallas_call(
        sort_gather,
        out_shape=jax.ShapeDtypeStruct((SPLIT, LANES), BF),
        in_specs=[whole()],
        out_specs=whole(),
        compiler_params=params(6),
        name="sort_gather",
    )(rows)
    gathered = lax.all_gather(gather_rows, LON, axis=0)
    spread_rows = pl.pallas_call(
        sort_spread,
        out_shape=jax.ShapeDtypeStruct((8, FFW - SPLIT, LANES), BF),
        in_specs=[whole(), pl.BlockSpec(memory_space=pl.ANY)],
        out_specs=pl.BlockSpec(memory_space=pl.ANY),
        scratch_shapes=[pltpu.VMEM((FFW - SPLIT, LANES), BF), pltpu.SemaphoreType.DMA((8,))],
        compiler_params=params(6),
        name="sort_spread",
    )(rows, gather_rows)
    near = lax.all_to_all(spread_rows, CHIPS, 0, 0)
    head_w = pl.pallas_call(
        sort_head,
        out_shape=jax.ShapeDtypeStruct((D, 2 * LANES), BF),
        in_specs=[whole()],
        out_specs=whole(),
        compiler_params=params(6),
        name="sort_head",
    )(rows)
    halo = jax.ShapeDtypeStruct((LANES, 4 * LANES), BF)
    keys = STRIPES * TOK
    q_t, k_n, v_t, to_up, to_down, bias = pl.pallas_call(
        project,
        out_shape=(
            jax.ShapeDtypeStruct((HEAD, keys), BF),
            jax.ShapeDtypeStruct((keys, HEAD), BF),
            jax.ShapeDtypeStruct((HEAD, keys), BF),
            halo,
            halo,
            jax.ShapeDtypeStruct((STRIPES, keys), F32),
        ),
        in_specs=[whole()] * 2,
        out_specs=(whole(),) * 6,
        compiler_params=params(14),
        cost_estimate=pl.CostEstimate(flops=2 * 2048 * 768 * 256, bytes_accessed=5 << 20, transcendentals=0),
        name="project",
    )(strip, head_w)
    above = lax.ppermute(to_down, LAT, [(i, i + 1) for i in range(31)])
    below = lax.ppermute(to_up, LAT, [(i + 1, i) for i in range(31)])

    stat = jax.ShapeDtypeStruct((8, keys), F32)
    acc, peaks, sums = pl.pallas_call(
        attend_strip,
        out_shape=(jax.ShapeDtypeStruct((HEAD, keys), F32), stat, stat),
        in_specs=[whole()] * 4,
        out_specs=(whole(),) * 3,
        scratch_shapes=[
            pltpu.VMEM((8, WIDE, WIDE), F32),
            pltpu.VMEM((8, WIDE, WIDE), F32),
            pltpu.VMEM((8, WIDE), F32),
            pltpu.VMEM((8, WIDE), F32),
        ],
        compiler_params=params(14),
        cost_estimate=pl.CostEstimate(
            flops=4 * 2048 * 2048 * 256, bytes_accessed=3 << 20, transcendentals=2048 * 2048
        ),
        name="attend_strip",
    )(q_t, k_n, v_t, bias)

    context = pl.pallas_call(
        attend_edges,
        out_shape=jax.ShapeDtypeStruct((STRIPES, HEAD, TOK), BF),
        in_specs=[whole()] * 6,
        out_specs=whole(),
        compiler_params=params(8),
        name="attend_edges",
    )(q_t, above, below, acc, peaks, sums)

    near, context = lax.optimization_barrier((near, context))
    far = lax.ppermute(near, "c", [(0, 1), (1, 0)])
    mine = lax.all_to_all(context, LON, 0, 0)
    mixed = pl.pallas_call(
        finish,
        out_shape=jax.ShapeDtypeStruct((TOK, D), BF),
        in_specs=[whole()] + [pl.BlockSpec(memory_space=pl.ANY)] * 3 + [whole()] * 3,
        out_specs=whole(),
        scratch_shapes=[pltpu.VMEM((STRIPES, FFW, LANES), BF), pltpu.SemaphoreType.DMA((32,))],
        compiler_params=params(56),
        cost_estimate=pl.CostEstimate(flops=2 * 128 * 768 * 3840, bytes_accessed=7 << 20, transcendentals=128 * 1536),
        name="finish",
    )(mine, gathered, near, far, own, patch_valid.reshape(TOK, 1), gain_mlp)
    return mixed.reshape(lat_rows, lon_cols, D)


def solution(mesh):
    fine = Mesh(mesh.devices.reshape(4, 2, 2, 2, 16), ("y", "xl", "c", "xh", "z"))
    in_specs = (
        P(LAT, LON, None),
        P(LAT, LON),
        P(LAT, LON, None),
        P(),
        P(),
        P(LAT, None),
        P(LAT, None),
        P(LAT, None),
        P(LAT, None),
    )
    out_specs = P(LAT, LON, None)
    return jax.shard_map(body, mesh=fine, in_specs=in_specs, out_specs=out_specs, check_vma=False)
```

```python
import functools

import jax
import jax.numpy as jnp
from jax import lax
from jax.experimental import pallas as pl
from jax.experimental.pallas import tpu as pltpu
from jax.sharding import Mesh, PartitionSpec as P

D = 768
HEADS = 12
HEAD = 64
FFW = 1536
TOK = 128
STRIPES = 16
LANES = 128
EDGE = 32
WIDE = 256
SPLIT = 528
MASKED = -1e30
LON = ("y", "xl", "c")
CHIPS = ("y", "xl")
LAT = ("xh", "z")
BF = jnp.bfloat16
F32 = jnp.float32


def norm_rows(x, gain):
    centre = jnp.mean(x, axis=-1, keepdims=True)
    diff = x - centre
    spread = jnp.mean(diff * diff, axis=-1, keepdims=True)
    return diff * lax.rsqrt(spread + 1e-05) * gain


def params(mib):
    return pltpu.CompilerParams(vmem_limit_bytes=mib << 20)


def whole():
    return pl.BlockSpec(memory_space=pltpu.VMEM)


def lon_place():
    return (lax.axis_index("y") * 2 + lax.axis_index("xl")) * 2 + lax.axis_index("c")


def prepare(tokens_ref, gain_ref, mask_ref, qkv_ref, out_ref, up_ref, down_ref, norm_out, piece_out):
    norm_out[pl.ds(0, TOK), :] = norm_rows(
        tokens_ref[...].astype(F32), gain_ref[...].reshape(1, D)
    ).astype(BF)
    seen = jnp.broadcast_to(mask_ref[0].astype(F32), (8, STRIPES))
    norm_out[pl.ds(TOK, 8), :] = jnp.concatenate([seen, jnp.zeros((8, D - STRIPES), F32)], axis=1).astype(BF)

    place_j = lon_place()
    head = lax.rem(place_j, HEADS)
    block = head // 2
    odd = lax.rem(head, 2) == 1
    parts = []
    for which in range(3):
        start = pl.multiple_of(which * D + block * LANES, LANES)
        pair = qkv_ref[:, pl.ds(start, LANES)].astype(F32)
        parts.append(jnp.where(odd, pltpu.roll(pair, HEAD, 1), pair))
    low = lax.broadcasted_iota(jnp.int32, (24, LANES), 1) < HEAD
    qk = jnp.where(low, parts[0], pltpu.roll(parts[1], HEAD, 1)).astype(BF)
    v = jnp.where(low, parts[2], 0.0).astype(BF)
    piece_out[pl.ds(0, 24), :] = qk
    piece_out[pl.ds(24, 24), :] = v

    def fill(top, bottom):
        piece_out[pl.ds(48, 24), :] = top
        piece_out[pl.ds(72, 24), :] = bottom

    @pl.when(place_j < 6)
    def _():
        span = pl.ds(pl.multiple_of(place_j * LANES, LANES), LANES)
        fill(down_ref[pl.ds(0, 24), span], down_ref[pl.ds(24, 24), span])

    @pl.when((place_j >= 6) & (place_j < 9))
    def _():
        start = pl.multiple_of((place_j - 6) * 2 * LANES, LANES)
        fill(out_ref[:, pl.ds(start, LANES)], out_ref[:, pl.ds(start + LANES, LANES)])

    @pl.when(place_j >= 9)
    def _():
        start = pl.multiple_of(jnp.minimum(place_j - 9, 5) * 2 * LANES, LANES)
        fill(up_ref[:, pl.ds(start, LANES)], up_ref[:, pl.ds(start + LANES, LANES)])


def sort_gather(rows_ref, gather_out):
    place_j = lon_place()
    xh = lax.axis_index("xh")

    @pl.when(place_j < 6)
    def _():
        for part in range(SPLIT // 48):
            gather_out[pl.ds(part * 48, 48), :] = rows_ref[part % 16, xh, pl.ds(48, 48), :]

    @pl.when(place_j >= 6)
    def _():
        for part in range(SPLIT // 24):
            source = rows_ref.at[part % 16, (part // 16) ^ xh]
            gather_out[pl.ds(part * 24, 24), :] = source[pl.ds(48, 24), :]


def sort_spread(rows_ref, order_ref, spread_hbm, rest, sems):
    place_j = lon_place()
    xh = lax.axis_index("xh")

    @pl.when(place_j < 6)
    def _():
        for part in range(SPLIT // 48, 32):
            source = rows_ref.at[part % 16, (part // 16) ^ xh]
            rest[pl.ds(part * 48 - SPLIT, 48), :] = source[pl.ds(48, 48), :]

    @pl.when(place_j >= 6)
    def _():
        for part in range(32):
            source = rows_ref.at[part % 16, (part // 16) ^ xh]
            if part * 24 >= SPLIT:
                rest[pl.ds(part * 24 - SPLIT, 24), :] = source[pl.ds(48, 24), :]
            rest[pl.ds(D - SPLIT + part * 24, 24), :] = source[pl.ds(72, 24), :]

    copies = [pltpu.make_async_copy(rest, spread_hbm.at[peer], sems.at[peer]) for peer in range(8)]
    for copy in copies:
        copy.start()
    for copy in copies:
        copy.wait()


def sort_head(rows_ref, head_out):
    xh = lax.axis_index("xh")
    for part in range(32):
        source = rows_ref.at[part % 16, (part // 16) ^ xh]
        head_out[pl.ds(part * 24, 24), pl.ds(0, LANES)] = source[pl.ds(0, 24), :]
        head_out[pl.ds(part * 24, 24), pl.ds(LANES, LANES)] = source[pl.ds(24, 24), :]


def project(strip_ref, weight_ref, q_out, k_out, vt_out, up_out, down_out, bias_out):
    weight = weight_ref[...]
    tops = []
    ends = []
    for tile in range(STRIPES):
        full = jnp.dot(strip_ref[tile, pl.ds(0, TOK), :], weight, preferred_element_type=F32)
        qk = full[:, :LANES]
        qk_t = jnp.transpose(qk)
        v_t = jnp.transpose(full[:, LANES:])[:HEAD]
        span = pl.ds(tile * TOK, TOK)
        q_out[:, span] = (qk_t[:HEAD] * HEAD ** (-0.5)).astype(BF)
        k_out[span, :] = qk[:, HEAD:].astype(BF)
        vt_out[:, span] = v_t.astype(BF)
        kv_t = jnp.concatenate([qk_t[HEAD:], v_t], axis=0)
        seen = jnp.broadcast_to(strip_ref[tile, pl.ds(TOK, 8), :LANES].astype(F32)[:1], (LANES, LANES))
        bias_out[:, span] = jnp.where(jnp.transpose(seen)[:STRIPES] > 0, 0.0, MASKED)
        tops.append(kv_t[:, :EDGE])
        ends.append(kv_t[:, TOK - EDGE :])
    for group in range(4):
        span = pl.ds(group * LANES, LANES)
        up_out[:, span] = jnp.concatenate(tops[group * 4 : group * 4 + 4], axis=1).astype(BF)
        down_out[:, span] = jnp.concatenate(ends[group * 4 : group * 4 + 4], axis=1).astype(BF)


def attend_strip(
    q_ref, k_ref, vt_ref, bias_ref, acc_out, max_out, sum_out, even_scores, odd_scores, even_top, odd_top
):
    def score_chunk(group, chunk, scores, top):
        span = pl.ds(pl.multiple_of(group * WIDE, WIDE), WIDE)
        part = jnp.dot(k_ref[pl.ds(chunk * WIDE, WIDE), :], q_ref[:, span], preferred_element_type=F32)
        for half in range(2):
            row = bias_ref[pl.ds(chunk * 2 + half, 1), span]
            piece = part[half * TOK : (half + 1) * TOK] + row
            scores[chunk, pl.ds(half * TOK, TOK), :] = piece
            best = jnp.max(piece.reshape(16, 8, WIDE), axis=0)
            top = best if top is None else jnp.maximum(top, best)
        return top

    def step(group, scores, top_ref, coming, next_scores, next_top):
        peak = jnp.max(top_ref[...], axis=0, keepdims=True)
        total = jnp.zeros((8, WIDE), F32)
        acc = jnp.zeros((HEAD, WIDE), F32)
        top = None
        for chunk in range(8):
            top = score_chunk(coming, chunk, next_scores, top)
            weights = jnp.exp(scores[chunk] - peak)
            total = total + jnp.sum(weights.reshape(32, 8, WIDE), axis=0)
            acc = acc + jnp.dot(
                vt_ref[:, pl.ds(chunk * WIDE, WIDE)], weights.astype(BF), preferred_element_type=F32
            )
        next_top[...] = top
        span = pl.ds(pl.multiple_of(group * WIDE, WIDE), WIDE)
        acc_out[:, span] = acc
        max_out[:, span] = jnp.broadcast_to(peak, (8, WIDE))
        sum_out[:, span] = jnp.broadcast_to(jnp.sum(total, axis=0, keepdims=True), (8, WIDE))

    top = None
    for chunk in range(8):
        top = score_chunk(0, chunk, even_scores, top)
    even_top[...] = top

    def pair(index, carry):
        first = index * 2
        step(first, even_scores, even_top, first + 1, odd_scores, odd_top)
        step(first + 1, odd_scores, odd_top, jnp.minimum(first + 2, 7), even_scores, even_top)
        return carry

    lax.fori_loop(0, 4, pair, 0)


def attend_edges(q_ref, above_ref, below_ref, acc_ref, max_ref, sum_ref, out_ref):
    row = lax.axis_index("xh") * 16 + lax.axis_index("z")
    key_band = lax.broadcasted_iota(jnp.int32, (LANES, 4 * TOK), 0) // EDGE
    query_band = lax.broadcasted_iota(jnp.int32, (LANES, 4 * TOK), 1) // TOK
    same = key_band == query_band
    for group in range(4):
        wide = slice(group * 4 * TOK, (group + 1) * 4 * TOK)
        keys = slice(group * LANES, (group + 1) * LANES)
        queries = q_ref[:, wide]
        scores = []
        for ref, flag in ((above_ref, row > 0), (below_ref, row < 31)):
            part = lax.dot_general(
                ref[:HEAD, keys], queries, (((0,), (0,)), ((), ())), preferred_element_type=F32
            )
            scores.append(jnp.where(same & flag, part, MASKED))
        old = max_ref[:1, wide]
        peak = jnp.maximum(old, jnp.max(jnp.maximum(scores[0], scores[1]), axis=0, keepdims=True))
        factor = jnp.exp(old - peak)
        acc = acc_ref[:, wide] * factor
        total = sum_ref[:1, wide] * factor
        for ref, part in ((above_ref, scores[0]), (below_ref, scores[1])):
            weights = jnp.exp(part - peak)
            total = total + jnp.sum(weights, axis=0, keepdims=True)
            acc = acc + jnp.dot(ref[HEAD:, keys], weights.astype(BF), preferred_element_type=F32)
        result = (acc / total).astype(BF)
        for index in range(4):
            out_ref[group * 4 + index] = result[:, index * TOK : (index + 1) * TOK]


def finish(
    ctx_ref, gather_hbm, near_ref, far_ref, tokens_ref, valid_ref, gain_ref, out_ref, gather_ref, sems
):
    core = lax.axis_index("c")
    order = (6, 7, 8, 9, 10, 11, 12, 13, 14, 0, 1, 2, 3, 4, 5)

    def piece(part):
        return pltpu.make_async_copy(gather_hbm.at[part], gather_ref.at[part], sems.at[part])

    for part in order:
        piece(part).start()

    def run(even_ref, odd_ref):
        context_t = ctx_ref[pl.ds(0, HEADS)].reshape(D, TOK)
        context = jnp.transpose(context_t.astype(F32)).astype(BF)
        valid = valid_ref[...].astype(F32)

        def column(part):
            ref = odd_ref if part % 2 else even_ref
            piece(part).wait()
            return [gather_ref[part], ref[part // 2]]

        def into(rows, part):
            head, rest = column(part)
            left = jnp.concatenate([head, rest[: D - SPLIT]], axis=0)
            weight = jnp.concatenate([left, rest[D - SPLIT :]], axis=1)
            return jnp.dot(rows, weight, preferred_element_type=F32)

        attended = jnp.concatenate([into(context, part) for part in range(6, 9)], axis=1)
        hidden = (tokens_ref[...].astype(F32) + valid * attended).astype(BF)
        residual = hidden.astype(F32)
        normed = norm_rows(residual, gain_ref[...].reshape(1, D)).astype(BF)
        inner = jnp.concatenate([jax.nn.gelu(into(normed, part)).astype(BF) for part in range(9, 15)], axis=1)
        for chunk in range(3):
            weight = jnp.concatenate(
                [jnp.concatenate(column(2 * chunk + side), axis=0) for side in range(2)], axis=1
            )
            down = jnp.dot(inner, weight, preferred_element_type=F32)
            span = slice(chunk * WIDE, (chunk + 1) * WIDE)
            out_ref[:, span] = (residual[:, span] + valid * down).astype(BF)

    @pl.when(core == 0)
    def _():
        run(near_ref, far_ref)

    @pl.when(core == 1)
    def _():
        run(far_ref, near_ref)


def body(tokens, patch_valid, block_mask, gain_attn, gain_mlp, w_qkv, w_out, w_up, w_down):
    lat_rows, lon_cols = tokens.shape[0], tokens.shape[1]
    own = tokens.reshape(TOK, D)
    normed, piece = pl.pallas_call(
        prepare,
        out_shape=(
            jax.ShapeDtypeStruct((TOK + 8, D), BF),
            jax.ShapeDtypeStruct((96, LANES), BF),
        ),
        in_specs=[whole()] * 7,
        out_specs=(whole(),) * 2,
        compiler_params=params(56),
        name="prepare",
    )(own, gain_attn, block_mask, w_qkv, w_out, w_up, w_down)
    twin = lax.ppermute(piece, "xh", [(0, 1), (1, 0)])
    strip = lax.all_gather(normed, LON, axis=0)
    both = jnp.stack([piece, twin])
    rows = lax.all_gather(both, "z", axis=0)
    gather_rows = pl.pallas_call(
        sort_gather,
        out_shape=jax.ShapeDtypeStruct((SPLIT, LANES), BF),
        in_specs=[whole()],
        out_specs=whole(),
        compiler_params=params(6),
        name="sort_gather",
    )(rows)
    gathered = lax.all_gather(gather_rows, LON, axis=0)
    spread_rows = pl.pallas_call(
        sort_spread,
        out_shape=jax.ShapeDtypeStruct((8, FFW - SPLIT, LANES), BF),
        in_specs=[whole(), pl.BlockSpec(memory_space=pl.ANY)],
        out_specs=pl.BlockSpec(memory_space=pl.ANY),
        scratch_shapes=[pltpu.VMEM((FFW - SPLIT, LANES), BF), pltpu.SemaphoreType.DMA((8,))],
        compiler_params=params(6),
        name="sort_spread",
    )(rows, gather_rows)
    near = lax.all_to_all(spread_rows, CHIPS, 0, 0)
    head_w = pl.pallas_call(
        sort_head,
        out_shape=jax.ShapeDtypeStruct((D, 2 * LANES), BF),
        in_specs=[whole()],
        out_specs=whole(),
        compiler_params=params(6),
        name="sort_head",
    )(rows)
    halo = jax.ShapeDtypeStruct((LANES, 4 * LANES), BF)
    keys = STRIPES * TOK
    q_t, k_n, v_t, to_up, to_down, bias = pl.pallas_call(
        project,
        out_shape=(
            jax.ShapeDtypeStruct((HEAD, keys), BF),
            jax.ShapeDtypeStruct((keys, HEAD), BF),
            jax.ShapeDtypeStruct((HEAD, keys), BF),
            halo,
            halo,
            jax.ShapeDtypeStruct((STRIPES, keys), F32),
        ),
        in_specs=[whole()] * 2,
        out_specs=(whole(),) * 6,
        compiler_params=params(14),
        cost_estimate=pl.CostEstimate(flops=2 * 2048 * 768 * 256, bytes_accessed=5 << 20, transcendentals=0),
        name="project",
    )(strip, head_w)
    above = lax.ppermute(to_down, LAT, [(i, i + 1) for i in range(31)])
    below = lax.ppermute(to_up, LAT, [(i + 1, i) for i in range(31)])

    stat = jax.ShapeDtypeStruct((8, keys), F32)
    acc, peaks, sums = pl.pallas_call(
        attend_strip,
        out_shape=(jax.ShapeDtypeStruct((HEAD, keys), F32), stat, stat),
        in_specs=[whole()] * 4,
        out_specs=(whole(),) * 3,
        scratch_shapes=[
            pltpu.VMEM((8, WIDE, WIDE), F32),
            pltpu.VMEM((8, WIDE, WIDE), F32),
            pltpu.VMEM((8, WIDE), F32),
            pltpu.VMEM((8, WIDE), F32),
        ],
        compiler_params=params(14),
        cost_estimate=pl.CostEstimate(
            flops=4 * 2048 * 2048 * 256, bytes_accessed=3 << 20, transcendentals=2048 * 2048
        ),
        name="attend_strip",
    )(q_t, k_n, v_t, bias)

    context = pl.pallas_call(
        attend_edges,
        out_shape=jax.ShapeDtypeStruct((STRIPES, HEAD, TOK), BF),
        in_specs=[whole()] * 6,
        out_specs=whole(),
        compiler_params=params(8),
        name="attend_edges",
    )(q_t, above, below, acc, peaks, sums)

    near, context = lax.optimization_barrier((near, context))
    far = lax.ppermute(near, "c", [(0, 1), (1, 0)])
    mine = lax.all_to_all(context, LON, 0, 0)
    mixed = pl.pallas_call(
        finish,
        out_shape=jax.ShapeDtypeStruct((TOK, D), BF),
        in_specs=[whole(), pl.BlockSpec(memory_space=pl.ANY)] + [whole()] * 5,
        out_specs=whole(),
        scratch_shapes=[pltpu.VMEM((STRIPES, SPLIT, LANES), BF), pltpu.SemaphoreType.DMA((15,))],
        compiler_params=params(51),
        cost_estimate=pl.CostEstimate(flops=2 * 128 * 768 * 3840, bytes_accessed=7 << 20, transcendentals=128 * 1536),
        name="finish",
    )(mine, gathered, near, far, own, patch_valid.reshape(TOK, 1), gain_mlp)
    return mixed.reshape(lat_rows, lon_cols, D)


def solution(mesh):
    fine = Mesh(mesh.devices.reshape(4, 2, 2, 2, 16), ("y", "xl", "c", "xh", "z"))
    in_specs = (
        P(LAT, LON, None),
        P(LAT, LON),
        P(LAT, LON, None),
        P(),
        P(),
        P(LAT, None),
        P(LAT, None),
        P(LAT, None),
        P(LAT, None),
    )
    out_specs = P(LAT, LON, None)
    return jax.shard_map(body, mesh=fine, in_specs=in_specs, out_specs=out_specs, check_vma=False)
```

```python
import functools

import jax
import jax.numpy as jnp
from jax import lax
from jax.experimental import pallas as pl
from jax.experimental.pallas import tpu as pltpu
from jax.sharding import Mesh, PartitionSpec as P

D = 768
HEADS = 12
HEAD = 64
FFW = 1536
TOK = 128
STRIPES = 16
LANES = 128
EDGE = 32
WIDE = 256
SPLIT = 720
MASKED = -1e30
LON = ("y", "xl", "c")
CHIPS = ("y", "xl")
LAT = ("xh", "z")
BF = jnp.bfloat16
F32 = jnp.float32


def norm_rows(x, gain):
    centre = jnp.mean(x, axis=-1, keepdims=True)
    diff = x - centre
    spread = jnp.mean(diff * diff, axis=-1, keepdims=True)
    return diff * lax.rsqrt(spread + 1e-05) * gain


def params(mib):
    return pltpu.CompilerParams(vmem_limit_bytes=mib << 20)


def whole():
    return pl.BlockSpec(memory_space=pltpu.VMEM)


def lon_place():
    return (lax.axis_index("y") * 2 + lax.axis_index("xl")) * 2 + lax.axis_index("c")


def prepare(tokens_ref, gain_ref, mask_ref, qkv_ref, out_ref, up_ref, down_ref, norm_out, piece_out):
    norm_out[pl.ds(0, TOK), :] = norm_rows(
        tokens_ref[...].astype(F32), gain_ref[...].reshape(1, D)
    ).astype(BF)
    seen = jnp.broadcast_to(mask_ref[0].astype(F32), (8, STRIPES))
    norm_out[pl.ds(TOK, 8), :] = jnp.concatenate([seen, jnp.zeros((8, D - STRIPES), F32)], axis=1).astype(BF)

    place_j = lon_place()
    head = lax.rem(place_j, HEADS)
    block = head // 2
    odd = lax.rem(head, 2) == 1
    parts = []
    for which in range(3):
        start = pl.multiple_of(which * D + block * LANES, LANES)
        pair = qkv_ref[:, pl.ds(start, LANES)].astype(F32)
        parts.append(jnp.where(odd, pltpu.roll(pair, HEAD, 1), pair))
    low = lax.broadcasted_iota(jnp.int32, (24, LANES), 1) < HEAD
    qk = jnp.where(low, parts[0], pltpu.roll(parts[1], HEAD, 1)).astype(BF)
    v = jnp.where(low, parts[2], 0.0).astype(BF)
    piece_out[pl.ds(0, 24), :] = qk
    piece_out[pl.ds(24, 24), :] = v

    def fill(top, bottom):
        piece_out[pl.ds(48, 24), :] = top
        piece_out[pl.ds(72, 24), :] = bottom

    @pl.when(place_j < 6)
    def _():
        span = pl.ds(pl.multiple_of(place_j * LANES, LANES), LANES)
        fill(down_ref[pl.ds(0, 24), span], down_ref[pl.ds(24, 24), span])

    @pl.when((place_j >= 6) & (place_j < 9))
    def _():
        start = pl.multiple_of((place_j - 6) * 2 * LANES, LANES)
        fill(out_ref[:, pl.ds(start, LANES)], out_ref[:, pl.ds(start + LANES, LANES)])

    @pl.when(place_j >= 9)
    def _():
        start = pl.multiple_of(jnp.minimum(place_j - 9, 5) * 2 * LANES, LANES)
        fill(up_ref[:, pl.ds(start, LANES)], up_ref[:, pl.ds(start + LANES, LANES)])


def sort_gather(rows_ref, gather_out):
    place_j = lon_place()
    xh = lax.axis_index("xh")

    @pl.when(place_j < 6)
    def _():
        for part in range(SPLIT // 48):
            gather_out[pl.ds(part * 48, 48), :] = rows_ref[part % 16, xh, pl.ds(48, 48), :]

    @pl.when(place_j >= 6)
    def _():
        for part in range(SPLIT // 24):
            source = rows_ref.at[part % 16, (part // 16) ^ xh]
            gather_out[pl.ds(part * 24, 24), :] = source[pl.ds(48, 24), :]


def sort_spread(rows_ref, order_ref, spread_hbm, rest, sems):
    place_j = lon_place()
    xh = lax.axis_index("xh")

    @pl.when(place_j < 6)
    def _():
        for part in range(SPLIT // 48, 32):
            source = rows_ref.at[part % 16, (part // 16) ^ xh]
            rest[pl.ds(part * 48 - SPLIT, 48), :] = source[pl.ds(48, 48), :]

    @pl.when(place_j >= 6)
    def _():
        for part in range(32):
            source = rows_ref.at[part % 16, (part // 16) ^ xh]
            if part * 24 >= SPLIT:
                rest[pl.ds(part * 24 - SPLIT, 24), :] = source[pl.ds(48, 24), :]
            rest[pl.ds(D - SPLIT + part * 24, 24), :] = source[pl.ds(72, 24), :]

    copies = [pltpu.make_async_copy(rest, spread_hbm.at[peer], sems.at[peer]) for peer in range(8)]
    for copy in copies:
        copy.start()
    for copy in copies:
        copy.wait()


def sort_head(rows_ref, head_out):
    xh = lax.axis_index("xh")
    for part in range(32):
        source = rows_ref.at[part % 16, (part // 16) ^ xh]
        head_out[pl.ds(part * 24, 24), pl.ds(0, LANES)] = source[pl.ds(0, 24), :]
        head_out[pl.ds(part * 24, 24), pl.ds(LANES, LANES)] = source[pl.ds(24, 24), :]


def project(strip_ref, weight_ref, q_out, k_out, vt_out, up_out, down_out, bias_out):
    weight = weight_ref[...]
    tops = []
    ends = []
    for tile in range(STRIPES):
        full = jnp.dot(strip_ref[tile, pl.ds(0, TOK), :], weight, preferred_element_type=F32)
        qk = full[:, :LANES]
        qk_t = jnp.transpose(qk)
        v_t = jnp.transpose(full[:, LANES:])[:HEAD]
        span = pl.ds(tile * TOK, TOK)
        q_out[:, span] = (qk_t[:HEAD] * HEAD ** (-0.5)).astype(BF)
        k_out[span, :] = qk[:, HEAD:].astype(BF)
        vt_out[:, span] = v_t.astype(BF)
        kv_t = jnp.concatenate([qk_t[HEAD:], v_t], axis=0)
        seen = jnp.broadcast_to(strip_ref[tile, pl.ds(TOK, 8), :LANES].astype(F32)[:1], (LANES, LANES))
        bias_out[:, span] = jnp.where(jnp.transpose(seen)[:STRIPES] > 0, 0.0, MASKED)
        tops.append(kv_t[:, :EDGE])
        ends.append(kv_t[:, TOK - EDGE :])
    for group in range(4):
        span = pl.ds(group * LANES, LANES)
        up_out[:, span] = jnp.concatenate(tops[group * 4 : group * 4 + 4], axis=1).astype(BF)
        down_out[:, span] = jnp.concatenate(ends[group * 4 : group * 4 + 4], axis=1).astype(BF)


def attend_strip(
    q_ref, k_ref, vt_ref, bias_ref, acc_out, max_out, sum_out, even_scores, odd_scores, even_top, odd_top
):
    def score_chunk(group, chunk, scores, top):
        span = pl.ds(pl.multiple_of(group * WIDE, WIDE), WIDE)
        part = jnp.dot(k_ref[pl.ds(chunk * WIDE, WIDE), :], q_ref[:, span], preferred_element_type=F32)
        for half in range(2):
            row = bias_ref[pl.ds(chunk * 2 + half, 1), span]
            piece = part[half * TOK : (half + 1) * TOK] + row
            scores[chunk, pl.ds(half * TOK, TOK), :] = piece
            best = jnp.max(piece.reshape(16, 8, WIDE), axis=0)
            top = best if top is None else jnp.maximum(top, best)
        return top

    def step(group, scores, top_ref, coming, next_scores, next_top):
        peak = jnp.max(top_ref[...], axis=0, keepdims=True)
        total = jnp.zeros((8, WIDE), F32)
        acc = jnp.zeros((HEAD, WIDE), F32)
        top = None
        for chunk in range(8):
            top = score_chunk(coming, chunk, next_scores, top)
            weights = jnp.exp(scores[chunk] - peak)
            total = total + jnp.sum(weights.reshape(32, 8, WIDE), axis=0)
            acc = acc + jnp.dot(
                vt_ref[:, pl.ds(chunk * WIDE, WIDE)], weights.astype(BF), preferred_element_type=F32
            )
        next_top[...] = top
        span = pl.ds(pl.multiple_of(group * WIDE, WIDE), WIDE)
        acc_out[:, span] = acc
        max_out[:, span] = jnp.broadcast_to(peak, (8, WIDE))
        sum_out[:, span] = jnp.broadcast_to(jnp.sum(total, axis=0, keepdims=True), (8, WIDE))

    top = None
    for chunk in range(8):
        top = score_chunk(0, chunk, even_scores, top)
    even_top[...] = top

    def pair(index, carry):
        first = index * 2
        step(first, even_scores, even_top, first + 1, odd_scores, odd_top)
        step(first + 1, odd_scores, odd_top, jnp.minimum(first + 2, 7), even_scores, even_top)
        return carry

    lax.fori_loop(0, 4, pair, 0)


def attend_edges(q_ref, above_ref, below_ref, acc_ref, max_ref, sum_ref, out_ref):
    row = lax.axis_index("xh") * 16 + lax.axis_index("z")
    key_band = lax.broadcasted_iota(jnp.int32, (LANES, 4 * TOK), 0) // EDGE
    query_band = lax.broadcasted_iota(jnp.int32, (LANES, 4 * TOK), 1) // TOK
    same = key_band == query_band
    for group in range(4):
        wide = slice(group * 4 * TOK, (group + 1) * 4 * TOK)
        keys = slice(group * LANES, (group + 1) * LANES)
        queries = q_ref[:, wide]
        scores = []
        for ref, flag in ((above_ref, row > 0), (below_ref, row < 31)):
            part = lax.dot_general(
                ref[:HEAD, keys], queries, (((0,), (0,)), ((), ())), preferred_element_type=F32
            )
            scores.append(jnp.where(same & flag, part, MASKED))
        old = max_ref[:1, wide]
        peak = jnp.maximum(old, jnp.max(jnp.maximum(scores[0], scores[1]), axis=0, keepdims=True))
        factor = jnp.exp(old - peak)
        acc = acc_ref[:, wide] * factor
        total = sum_ref[:1, wide] * factor
        for ref, part in ((above_ref, scores[0]), (below_ref, scores[1])):
            weights = jnp.exp(part - peak)
            total = total + jnp.sum(weights, axis=0, keepdims=True)
            acc = acc + jnp.dot(ref[HEAD:, keys], weights.astype(BF), preferred_element_type=F32)
        result = (acc / total).astype(BF)
        for index in range(4):
            out_ref[group * 4 + index] = result[:, index * TOK : (index + 1) * TOK]


def finish(ctx_ref, gather_ref, near_ref, far_ref, tokens_ref, valid_ref, gain_ref, out_ref):
    core = lax.axis_index("c")

    def run(even_ref, odd_ref):
        context_t = ctx_ref[pl.ds(0, HEADS)].reshape(D, TOK)
        context = jnp.transpose(context_t.astype(F32)).astype(BF)
        valid = valid_ref[...].astype(F32)

        def column(part):
            ref = odd_ref if part % 2 else even_ref
            return [gather_ref[part], ref[part // 2]]

        def into(rows, part):
            head, rest = column(part)
            left = jnp.concatenate([head, rest[: D - SPLIT]], axis=0)
            weight = jnp.concatenate([left, rest[D - SPLIT :]], axis=1)
            return jnp.dot(rows, weight, preferred_element_type=F32)

        attended = jnp.concatenate([into(context, part) for part in range(6, 9)], axis=1)
        hidden = (tokens_ref[...].astype(F32) + valid * attended).astype(BF)
        residual = hidden.astype(F32)
        normed = norm_rows(residual, gain_ref[...].reshape(1, D)).astype(BF)
        inner = jnp.concatenate([jax.nn.gelu(into(normed, part)).astype(BF) for part in range(9, 15)], axis=1)
        for chunk in range(3):
            weight = jnp.concatenate(
                [jnp.concatenate(column(2 * chunk + side), axis=0) for side in range(2)], axis=1
            )
            down = jnp.dot(inner, weight, preferred_element_type=F32)
            span = slice(chunk * WIDE, (chunk + 1) * WIDE)
            out_ref[:, span] = (residual[:, span] + valid * down).astype(BF)

    @pl.when(core == 0)
    def _():
        run(near_ref, far_ref)

    @pl.when(core == 1)
    def _():
        run(far_ref, near_ref)


def body(tokens, patch_valid, block_mask, gain_attn, gain_mlp, w_qkv, w_out, w_up, w_down):
    lat_rows, lon_cols = tokens.shape[0], tokens.shape[1]
    own = tokens.reshape(TOK, D)
    normed, piece = pl.pallas_call(
        prepare,
        out_shape=(
            jax.ShapeDtypeStruct((TOK + 8, D), BF),
            jax.ShapeDtypeStruct((96, LANES), BF),
        ),
        in_specs=[whole()] * 7,
        out_specs=(whole(),) * 2,
        compiler_params=params(56),
        name="prepare",
    )(own, gain_attn, block_mask, w_qkv, w_out, w_up, w_down)
    twin = lax.ppermute(piece, "xh", [(0, 1), (1, 0)])
    strip = lax.all_gather(normed, LON, axis=0)
    both = jnp.stack([piece, twin])
    rows = lax.all_gather(both, "z", axis=0)
    gather_rows = pl.pallas_call(
        sort_gather,
        out_shape=jax.ShapeDtypeStruct((SPLIT, LANES), BF),
        in_specs=[whole()],
        out_specs=whole(),
        compiler_params=params(6),
        name="sort_gather",
    )(rows)
    gathered = lax.all_gather(gather_rows, LON, axis=0)
    spread_rows = pl.pallas_call(
        sort_spread,
        out_shape=jax.ShapeDtypeStruct((8, FFW - SPLIT, LANES), BF),
        in_specs=[whole(), pl.BlockSpec(memory_space=pl.ANY)],
        out_specs=pl.BlockSpec(memory_space=pl.ANY),
        scratch_shapes=[pltpu.VMEM((FFW - SPLIT, LANES), BF), pltpu.SemaphoreType.DMA((8,))],
        compiler_params=params(6),
        name="sort_spread",
    )(rows, gather_rows)
    near = lax.all_to_all(spread_rows, CHIPS, 0, 0)
    head_w = pl.pallas_call(
        sort_head,
        out_shape=jax.ShapeDtypeStruct((D, 2 * LANES), BF),
        in_specs=[whole()],
        out_specs=whole(),
        compiler_params=params(6),
        name="sort_head",
    )(rows)
    halo = jax.ShapeDtypeStruct((LANES, 4 * LANES), BF)
    keys = STRIPES * TOK
    q_t, k_n, v_t, to_up, to_down, bias = pl.pallas_call(
        project,
        out_shape=(
            jax.ShapeDtypeStruct((HEAD, keys), BF),
            jax.ShapeDtypeStruct((keys, HEAD), BF),
            jax.ShapeDtypeStruct((HEAD, keys), BF),
            halo,
            halo,
            jax.ShapeDtypeStruct((STRIPES, keys), F32),
        ),
        in_specs=[whole()] * 2,
        out_specs=(whole(),) * 6,
        compiler_params=params(14),
        cost_estimate=pl.CostEstimate(flops=2 * 2048 * 768 * 256, bytes_accessed=5 << 20, transcendentals=0),
        name="project",
    )(strip, head_w)
    above = lax.ppermute(to_down, LAT, [(i, i + 1) for i in range(31)])
    below = lax.ppermute(to_up, LAT, [(i + 1, i) for i in range(31)])

    stat = jax.ShapeDtypeStruct((8, keys), F32)
    acc, peaks, sums = pl.pallas_call(
        attend_strip,
        out_shape=(jax.ShapeDtypeStruct((HEAD, keys), F32), stat, stat),
        in_specs=[whole()] * 4,
        out_specs=(whole(),) * 3,
        scratch_shapes=[
            pltpu.VMEM((8, WIDE, WIDE), F32),
            pltpu.VMEM((8, WIDE, WIDE), F32),
            pltpu.VMEM((8, WIDE), F32),
            pltpu.VMEM((8, WIDE), F32),
        ],
        compiler_params=params(14),
        cost_estimate=pl.CostEstimate(
            flops=4 * 2048 * 2048 * 256, bytes_accessed=3 << 20, transcendentals=2048 * 2048
        ),
        name="attend_strip",
    )(q_t, k_n, v_t, bias)

    context = pl.pallas_call(
        attend_edges,
        out_shape=jax.ShapeDtypeStruct((STRIPES, HEAD, TOK), BF),
        in_specs=[whole()] * 6,
        out_specs=whole(),
        compiler_params=params(8),
        name="attend_edges",
    )(q_t, above, below, acc, peaks, sums)

    near, context = lax.optimization_barrier((near, context))
    far = lax.ppermute(near, "c", [(0, 1), (1, 0)])
    mine = lax.all_to_all(context, LON, 0, 0)
    mixed = pl.pallas_call(
        finish,
        out_shape=jax.ShapeDtypeStruct((TOK, D), BF),
        in_specs=[whole()] * 7,
        out_specs=whole(),
        compiler_params=params(20),
        cost_estimate=pl.CostEstimate(flops=2 * 128 * 768 * 3840, bytes_accessed=7 << 20, transcendentals=128 * 1536),
        name="finish",
    )(mine, gathered, near, far, own, patch_valid.reshape(TOK, 1), gain_mlp)
    return mixed.reshape(lat_rows, lon_cols, D)


def solution(mesh):
    fine = Mesh(mesh.devices.reshape(4, 2, 2, 2, 16), ("y", "xl", "c", "xh", "z"))
    in_specs = (
        P(LAT, LON, None),
        P(LAT, LON),
        P(LAT, LON, None),
        P(),
        P(),
        P(LAT, None),
        P(LAT, None),
        P(LAT, None),
        P(LAT, None),
    )
    out_specs = P(LAT, LON, None)
    return jax.shard_map(body, mesh=fine, in_specs=in_specs, out_specs=out_specs, check_vma=False)
```
